32 devices in a mesh: row: 8 (over y, x, core), col: 4 (over z).
Axes of the slice: x: 2, y: 2, z: 4, core: 2. Of those that a mesh axis runs over, the one named last changes fastest.
Arguments:
- dual_ops: float32 [8, 4, 2048, 2048], P('row', 'col'), as said below
- basis: float32 [8, 4, 4, 64, 512], P('row', 'col'), may hold values from -0.125 to 0.125
- coarse_inverse: float32 [2048, 2048], P('row', 'col')
- gap_rhs: float32 [8, 4, 4, 32, 512], P('row', 'col'), may hold values from -6 to 6
- coarse_rhs: float32 [8, 4, 32, 64], P('row', 'col'), may hold values from -6 to 6
- contact_mask: int32 [8, 4, 4, 512], P('row', 'col'), may hold values 0 or 1
Outputs:
- multipliers: float32 [8, 4, 4, 32, 512], P('row', 'col')
- projected_grad: float32 [8, 4, 4, 32, 512], P('row', 'col')
The draws below stay inside these ranges and needn't reach their ends.
Inputs may be any that keep to these rules, and one draw needn't show every extreme that they name: `dual_ops`: each subdomain's dual operator is symmetric and positive definite.
All inputs are finite; a program needn't handle non-finite values. No bound on the sum of `contact_mask` on one device may be relied on, other than what follows from the above.
Results may differ from the reference program's by a relative error of at most 0.00025.
Values sent between devices are 32-bit elements; how exact they have to be, the bound alone decides.
A program may use at most 128 MiB of HBM per device.

```python
import math
import jax
import jax.numpy as jnp
from jax import lax

M = 2048
FACE = 512
K = 32
MDEV = 64
NMODES = 2048
ITERS = 6
N_ROW = 8
N_COL = 4


def draw_dual_ops(key, part):
    keys = jax.random.split(key, N_ROW * N_COL)
    limit = 4.0 / math.sqrt(M)

    def single(subkey):
        raw = jax.random.normal(subkey, (M, M), jnp.float32)
        offdiag = (raw + raw.T) * (0.5 / math.sqrt(M))
        offdiag = jnp.clip(offdiag, -limit, limit) * (1.0 - jnp.eye(M, dtype=jnp.float32))
        return offdiag + 2.5 * jnp.eye(M, dtype=jnp.float32)
    return lax.map(single, keys).reshape(N_ROW, N_COL, M, M)


def draw_coarse_inverse(key, part):
    raw = jax.random.normal(key, (NMODES, NMODES), jnp.float32)
    return jnp.eye(NMODES, dtype=jnp.float32) + raw * (0.3 / math.sqrt(NMODES))


def set_ends(values, own_key, low, high):
    place = [jax.random.randint(jax.random.fold_in(own_key, axis), (), 0, length) for axis, length in enumerate(values.shape)]
    widest = values.shape.index(max(values.shape))
    neighbour = place[:widest] + [(place[widest] + 1) % values.shape[widest]] + place[widest + 1:]
    return values.at[tuple(place)].set(low).at[tuple(neighbour)].set(high)


def level_of(stream_key, dims, cuts, low, top_value):
    def one(position, blocks):
        heights = jax.random.uniform(jax.random.fold_in(jax.random.fold_in(stream_key, 6), position), (blocks,), jnp.float32, low / len(cuts), top_value / len(cuts))
        return jnp.repeat(jnp.exp(heights), dims[position] // blocks).reshape((-1,) + (1,) * (len(dims) - position - 1))

    factor_of = one(*cuts[0])
    for cut in cuts[1:]:
        factor_of = factor_of * one(*cut)
    return factor_of


def noise(key, dims, spread, most, pieces=(), held_as=jnp.bfloat16):
    drawn = jax.random.normal(key, dims, jnp.float32) * spread
    if len(pieces) > 0:
        drawn = level_of(key, dims, pieces, -0.22, 0.18) * drawn
    return jnp.clip(drawn, min=-most, max=most).astype(held_as)


def setup_inputs(seed: int = 0) -> dict:
    splits = jax.random.split(jax.random.key(seed), 7)
    return {
        "dual_ops": draw_dual_ops(jax.random.fold_in(splits[6], 71), 0),
        "basis": noise(splits[1], (N_ROW, N_COL, 4, MDEV, FACE), M ** -0.5, 0.125, ((0, 8), (1, 4)), jnp.float32),
        "coarse_inverse": draw_coarse_inverse(jax.random.fold_in(splits[6], 71), 0),
        "gap_rhs": noise(splits[3], (N_ROW, N_COL, 4, K, FACE), 1.0, 6.0, ((0, 8), (1, 4)), jnp.float32),
        "coarse_rhs": noise(splits[4], (N_ROW, N_COL, K, MDEV), 1.0, 6.0, ((0, 8), (1, 4)), jnp.float32),
        "contact_mask": set_ends((jax.random.randint(splits[5], (N_ROW, N_COL, 4, FACE), 0, 2) < 1).astype(jnp.int32), jax.random.fold_in(splits[5], 1), 0, 1),
    }


HIGH = lax.Precision.HIGHEST


def neighbour_faces(values):
    zero_row = jnp.zeros_like(values[:1, :, 0])
    zero_col = jnp.zeros_like(values[:, :1, 0])
    from_above = jnp.concatenate([zero_row, values[:-1, :, 1]], axis=0)
    from_below = jnp.concatenate([values[1:, :, 0], zero_row], axis=0)
    from_left = jnp.concatenate([zero_col, values[:, :-1, 3]], axis=1)
    from_right = jnp.concatenate([values[:, 1:, 2], zero_col], axis=1)
    return jnp.stack([from_above, from_below, from_left, from_right], axis=2)


def interface_sum(values):
    return values + neighbour_faces(values)


def reference(dual_ops, basis, coarse_inverse, gap_rhs, coarse_rhs, contact_mask):
    blocks = dual_ops.reshape(N_ROW, N_COL, 4, FACE, 4, FACE)

    def apply_dual(vector):
        return jnp.einsum("rcgjfi,rcfki->rcgkj", blocks, vector, precision=HIGH)

    def expand(amps):
        return jnp.einsum("rcfji,rckj->rcfki", basis, amps, precision=HIGH)

    def restrict(vector):
        return jnp.einsum("rcfji,rcfki->rckj", basis, vector, precision=HIGH)

    def coarse(coef):
        column_major = jnp.transpose(coef, (2, 1, 0, 3)).reshape(K, NMODES)
        amps = jnp.dot(column_major, coarse_inverse.T, precision=HIGH, preferred_element_type=jnp.float32)
        return jnp.transpose(amps.reshape(K, N_ROW, N_COL, MDEV), (1, 2, 0, 3))

    row_ids = jnp.arange(N_ROW)[:, None]
    col_ids = jnp.arange(N_COL)[None, :]
    has_nb = jnp.stack([
        jnp.broadcast_to(row_ids > 0, (N_ROW, N_COL)),
        jnp.broadcast_to(row_ids < N_ROW - 1, (N_ROW, N_COL)),
        jnp.broadcast_to(col_ids > 0, (N_ROW, N_COL)),
        jnp.broadcast_to(col_ids < N_COL - 1, (N_ROW, N_COL))], axis=2)
    weight = jnp.where(has_nb, 0.5, 1.0).astype(jnp.float32)[:, :, :, None, None]
    contact = jnp.logical_and(contact_mask == 1, jnp.logical_not(has_nb)[:, :, :, None])[:, :, :, None, :]

    dvec = interface_sum(gap_rhs)
    multipliers = interface_sum(expand(coarse(coarse_rhs)))
    projected = jnp.zeros_like(multipliers)
    for step in range(ITERS):
        grad = interface_sum(apply_dual(multipliers)) - dvec
        projected = grad - interface_sum(expand(coarse(restrict(grad))))
        image = apply_dual(projected)
        numer = jnp.sum(weight * grad * projected, axis=(0, 1, 2, 4))
        denom = jnp.sum(projected * image, axis=(0, 1, 2, 4))
        ratio = numer / denom
        multipliers = multipliers - ratio[None, None, None, :, None] * projected
        multipliers = jnp.where(contact, jnp.maximum(multipliers, 0.0), multipliers)
    return multipliers, projected
```

```python
import functools
import math

import jax
import jax.numpy as jnp
from jax import lax
from jax.experimental import pallas as pl
from jax.experimental.pallas import tpu as pltpu
from jax.sharding import PartitionSpec as P

ITERS = 6
MESH = pl.DeviceIdType.MESH
F32 = jnp.float32
BF16 = jnp.bfloat16


def split(x):
    hi = x.astype(BF16)
    return hi, (x - hi.astype(F32)).astype(BF16)


def dot(a, b, dims):
    return lax.dot_general(a, b, (dims, ((), ())), preferred_element_type=F32)


def dot3(x, hi, lo, dims):
    rows = x.shape[0]
    x_hi, x_lo = split(x)
    both = dot(jnp.concatenate([x_hi, x_lo], axis=0), hi, dims)
    return both[:rows] + (both[rows:] + dot(x_hi, lo, dims))


def pack(x):
    half = x.shape[0] // 2
    return jnp.concatenate([x[:half], x[half:]], axis=1)


def unpack(parts):
    n = parts[0].shape[1] // 2
    top = jnp.concatenate([p[:, :n] for p in parts], axis=1)
    return jnp.concatenate([top, jnp.concatenate([p[:, n:] for p in parts], axis=1)], axis=0)


def kernel(n_rows, n_cols, a_hbm, basis, cinv, gap, crhs, mask, m_out, p_out,
           stage, ahi, alo, bhi, blo, chi, clo, nbb, nbgap, halo_in, am, dvec, grad, image, xs, whi, wlo,
           ebuf, pout, pin, amp_s, nbamps, red,
           a_sem, bs, br, gs, gr, hs, hr, es, er, ps, pr, ams, amr, rs, rr):
    row = lax.axis_index("row")
    col = lax.axis_index("col")
    me = row * n_cols + col
    n_dev = n_rows * n_cols
    m_len = ahi.shape[0]
    _, k, face = halo_in.shape
    mdev = nbb.shape[1]
    width = red.shape[2]
    step_rows = m_len // a_sem.shape[0]
    n_blocks = a_sem.shape[0]
    has_nb = [row > 0, row < n_rows - 1, col > 0, col < n_cols - 1]
    nbr = [(row - 1, col), (row + 1, col), (row, col - 1), (row, col + 1)]

    def a_copy(i):
        rows = pl.ds(pl.multiple_of(i * step_rows, step_rows), step_rows)
        return pltpu.make_async_copy(a_hbm.at[0, 0, rows], stage.at[rows], a_sem.at[i])

    def a_start(i, carry):
        a_copy(i).start()
        return carry

    lax.fori_loop(0, n_blocks, a_start, 0)

    barrier = pltpu.get_barrier_semaphore()
    for d in range(1, n_dev):
        t = lax.rem(me + d, n_dev)
        pl.semaphore_signal(barrier, inc=1, device_id=(t // n_cols, lax.rem(t, n_cols)), device_id_type=MESH)
    pl.semaphore_wait(barrier, n_dev - 1)

    def remote(src, dst, ssem, rsem, where):
        return pltpu.make_async_remote_copy(
            src_ref=src, dst_ref=dst, send_sem=ssem, recv_sem=rsem, device_id=where, device_id_type=MESH)

    def face_start(f, src, dst, ssem, rsem):
        @pl.when(has_nb[f])
        def _():
            remote(src, dst.at[f ^ 1], ssem.at[f], rsem.at[f ^ 1], nbr[f]).start()

    def face_wait(f, src, dst, ssem, rsem):
        @pl.when(has_nb[f])
        def _():
            remote(src, dst.at[f], ssem.at[f], rsem.at[f], nbr[f]).wait()

    def basis_face(f):
        return basis.at[0, 0, f]

    def coarse(use, e, first=None, second=None, third=None):
        ebuf[use, row] = pack(e)
        copies = []
        for d in range(1, n_rows):
            copies.append(remote(ebuf.at[use, row], ebuf.at[use, row], es.at[use, d], er.at[use, d], (lax.rem(row + d, n_rows), col)))
            copies[-1].start()
        if first is not None:
            first()
        for copy in copies:
            copy.wait()
        gathered = unpack([ebuf[use, r] for r in range(n_rows)])
        partial = dot3(gathered, chi[...], clo[...], ((1,), (1,)))
        for c in range(n_cols):
            pout[c] = pack(partial[:, c * mdev:(c + 1) * mdev])
        copies = []
        for d in range(1, n_cols):
            c = lax.rem(col + d, n_cols)
            copies.append(remote(pout.at[c], pin.at[use, col], ps.at[use, d], pr.at[use, d], (row, c)))
            copies[-1].start()
        pin[use, col] = pout[col]
        if second is not None:
            second()
        for copy in copies:
            copy.wait()
        amps = pin[use, 0]
        for c in range(1, n_cols):
            amps = amps + pin[use, c]
        amp_s[...] = amps
        for f in range(4):
            face_start(f, amp_s, nbamps, ams, amr)
        if third is not None:
            third()
        for f in range(4):
            face_wait(f, amp_s, nbamps, ams, amr)
        return amps

    def expand_sum(amps, f):
        both = unpack([amps, nbamps[f]])
        return dot3(both, bhi[f], blo[f], ((1,), (0,)))

    def put_split(x, f):
        hi, lo = split(x)
        xs[0:k, f * face:(f + 1) * face] = hi
        xs[k:2 * k, f * face:(f + 1) * face] = lo

    def apply_face(f):
        cols = slice(f * face, (f + 1) * face)
        both = dot(xs[...], ahi[:, cols], ((1,), (0,)))
        low = dot(xs[0:k, :], alo[:, cols], ((1,), (0,)))
        return both[:k] + (both[k:] + low)

    for f in range(4):
        face_start(f, basis_face(f), nbb, bs, br)
        face_start(f, gap.at[0, 0, f], nbgap, gs, gr)
    zero_face = jnp.zeros((k, face), F32)
    for f in range(4):
        @pl.when(jnp.logical_not(has_nb[f]))
        def _():
            nbb[f] = jnp.zeros((mdev, face), F32)
            nbgap[f] = zero_face
            halo_in[f] = zero_face
            nbamps[f] = jnp.zeros((k // 2, 2 * mdev), F32)
    c_hi, c_lo = split(cinv[...])
    chi[...] = c_hi
    clo[...] = c_lo
    for f in range(4):
        hi, lo = split(basis[0, 0, f])
        bhi[f, 0:mdev] = hi
        blo[f, 0:mdev] = lo
    amps = coarse(0, crhs[0, 0])
    for f in range(4):
        face_wait(f, basis_face(f), nbb, bs, br)
        face_wait(f, gap.at[0, 0, f], nbgap, gs, gr)
        hi, lo = split(nbb[f])
        bhi[f, mdev:2 * mdev] = hi
        blo[f, mdev:2 * mdev] = lo
        dvec[f] = gap[0, 0, f] + nbgap[f]
        m = expand_sum(amps, f)
        m_out[0, 0, f] = m
        put_split(m, f)

    def a_split(i, carry):
        a_copy(i).wait()
        rows = pl.ds(pl.multiple_of(i * step_rows, step_rows), step_rows)
        hi, lo = split(stage[rows, :])
        ahi[rows, :] = hi
        alo[rows, :] = lo
        return carry

    lax.fori_loop(0, n_blocks, a_split, 0)

    lane = lax.broadcasted_iota(jnp.int32, (k, width), 1)
    sub = lax.broadcasted_iota(jnp.int32, (k, width), 0)

    own_hi = jnp.concatenate([bhi[f, 0:mdev] for f in range(4)], axis=1)
    own_lo = jnp.concatenate([blo[f, 0:mdev] for f in range(4)], axis=1)
    own = jnp.concatenate([own_hi, own_lo], axis=0)
    for g in range(4):
        cols = slice(g * face, (g + 1) * face)
        am[g] = apply_face(g)
        both = dot(own, ahi[:, cols], ((1,), (0,)))
        low = dot(own_hi, alo[:, cols], ((1,), (0,)))
        hi, lo = split(both[:mdev] + (both[mdev:] + low))
        whi[0:mdev, cols] = hi
        wlo[0:mdev, cols] = lo
        for f in range(4):
            rows = slice(f * face, (f + 1) * face)
            nb_hi, nb_lo = bhi[f, mdev:2 * mdev], blo[f, mdev:2 * mdev]
            both = dot(jnp.concatenate([nb_hi, nb_lo], axis=0), ahi[rows, cols], ((1,), (0,)))
            low = dot(nb_hi, alo[rows, cols], ((1,), (0,)))
            hi, lo = split(both[:mdev] + (both[mdev:] + low))
            whi[(f + 1) * mdev:(f + 2) * mdev, cols] = hi
            wlo[(f + 1) * mdev:(f + 2) * mdev, cols] = lo

    def all_sum():
        copies = []
        for d in range(1, n_dev):
            t = lax.rem(me + d, n_dev)
            copies.append(remote(red.at[me], red.at[me], rs.at[d], rr.at[d], (t // n_cols, lax.rem(t, n_cols))))
            copies[-1].start()
        for copy in copies:
            copy.wait()
        return jnp.sum(red[...], axis=0)

    def iteration(step, carry):
        for f in range(4):
            face_start(f, am.at[f], halo_in, hs, hr)
        e = jnp.zeros((k, mdev), F32)
        for f in range(4):
            face_wait(f, am.at[f], halo_in, hs, hr)
            g = am[f] + halo_in[f] - dvec[f]
            grad[f] = g
            put_split(g, f)
            e = e + dot3(g, bhi[f, 0:mdev], blo[f, 0:mdev], ((1,), (1,)))

        def first():
            image[0] = apply_face(0)
            image[1] = apply_face(1)

        def second():
            image[2] = apply_face(2)

        def third():
            image[3] = apply_face(3)

        amps = coarse(1, e, first, second, third)
        every = unpack([amps] + [nbamps[f] for f in range(4)])
        numer = jnp.zeros((k, 1), F32)
        denom = jnp.zeros((k, 1), F32)
        for f in range(4):
            cols = slice(f * face, (f + 1) * face)
            g = grad[f]
            p = g - expand_sum(amps, f)
            p_out[0, 0, f] = p
            weight = jnp.where(has_nb[f], 0.5, 1.0).astype(F32)
            numer = numer + weight * jnp.sum(g * p, axis=1, keepdims=True)
            im = image[f] - dot3(every, whi[:, cols], wlo[:, cols], ((1,), (0,)))
            image[f] = im
            denom = denom + jnp.sum(p * im, axis=1, keepdims=True)
        packed = jnp.where(lane == sub, numer, 0.0) + jnp.where(lane == sub + k, denom, 0.0)
        red[me] = jnp.sum(packed, axis=0, keepdims=True)
        total = all_sum()
        numer_all = jnp.sum(jnp.where(lane == sub, total, 0.0), axis=1, keepdims=True)
        denom_all = jnp.sum(jnp.where(lane == sub + k, total, 0.0), axis=1, keepdims=True)
        ratio = numer_all / denom_all
        for f in range(4):
            am[f] = am[f] - ratio * image[f]
            linear = m_out[0, 0, f] - ratio * p_out[0, 0, f]
            contact = jnp.where(has_nb[f], 0, mask[0, 0, f:f + 1, :])
            m = jnp.where(contact == 1, jnp.maximum(linear, 0.0), linear)
            m_out[0, 0, f] = m
            put_split(m - linear, f)
        for f in range(4):
            @pl.when(jnp.logical_and(jnp.logical_not(has_nb[f]), step < ITERS - 1))
            def _():
                rows = slice(f * face, (f + 1) * face)
                change = xs[:, rows]
                for g in range(4):
                    cols = slice(g * face, (g + 1) * face)
                    both = dot(change, ahi[rows, cols], ((1,), (0,)))
                    low = dot(change[0:k], alo[rows, cols], ((1,), (0,)))
                    am[g] = am[g] + (both[:k] + (both[k:] + low))
        return carry

    lax.fori_loop(0, ITERS, iteration, 0)


def solution(mesh):
    n_rows, n_cols = mesh.shape["row"], mesh.shape["col"]

    def shards(dual_ops, basis, coarse_inverse, gap_rhs, coarse_rhs, contact_mask):
        m_len = dual_ops.shape[-1]
        _, _, _, k, face = gap_rhs.shape
        mdev = basis.shape[3]
        width = -(-2 * k // 128) * 128
        blocks = math.gcd(m_len, 32)
        vm = pltpu.VMEM
        dma = pltpu.SemaphoreType.DMA
        small = (k // 2, 2 * mdev)
        faces = vm((4, k, face), F32)
        out = jax.ShapeDtypeStruct(gap_rhs.shape, F32)
        in_vmem = pl.BlockSpec(memory_space=pltpu.VMEM)
        return pl.pallas_call(
            functools.partial(kernel, n_rows, n_cols),
            out_shape=(out, out),
            in_specs=[pl.BlockSpec(memory_space=pl.ANY)] + [in_vmem] * 5,
            out_specs=(in_vmem, in_vmem),
            scratch_shapes=[
                vm((m_len, m_len), F32), vm((m_len, m_len), BF16), vm((m_len, m_len), BF16),
                vm((4, 2 * mdev, face), BF16), vm((4, 2 * mdev, face), BF16),
                vm(coarse_inverse.shape, BF16), vm(coarse_inverse.shape, BF16),
                vm((4, mdev, face), F32), faces, faces, faces, faces, faces, faces,
                vm((2 * k, m_len), BF16), vm((5 * mdev, m_len), BF16), vm((5 * mdev, m_len), BF16),
                vm((2, n_rows, *small), F32), vm((n_cols, *small), F32), vm((2, n_cols, *small), F32),
                vm(small, F32), vm((4, *small), F32), vm((n_rows * n_cols, 1, width), F32),
                dma((blocks,)),
                dma((4,)), dma((4,)), dma((4,)), dma((4,)), dma((4,)), dma((4,)),
                dma((2, n_rows)), dma((2, n_rows)), dma((2, n_cols)), dma((2, n_cols)),
                dma((4,)), dma((4,)), dma((n_rows * n_cols,)), dma((n_rows * n_cols,)),
            ],
            compiler_params=pltpu.CompilerParams(
                collective_id=0, has_side_effects=True, vmem_limit_bytes=60 * 1024 * 1024),
        )(dual_ops, basis, coarse_inverse, gap_rhs, coarse_rhs, contact_mask)

    return jax.shard_map(
        shards,
        mesh=mesh,
        in_specs=(
            P("row", "col", None, None),
            P("row", "col", None, None, None),
            P("row", "col"),
            P("row", "col", None, None, None),
            P("row", "col", None, None),
            P("row", "col", None, None),
        ),
        out_specs=(P("row", "col", None, None, None), P("row", "col", None, None, None)),
        check_vma=False,
    )
```

```python
import functools
import math

import jax
import jax.numpy as jnp
from jax import lax
from jax.experimental import pallas as pl
from jax.experimental.pallas import tpu as pltpu
from jax.sharding import PartitionSpec as P

ITERS = 6
MESH = pl.DeviceIdType.MESH
F32 = jnp.float32
BF16 = jnp.bfloat16


def split(x):
    hi = x.astype(BF16)
    return hi, (x - hi.astype(F32)).astype(BF16)


def dot(a, b, dims):
    return lax.dot_general(a, b, (dims, ((), ())), preferred_element_type=F32)


def dot3(x, hi, lo, dims):
    rows = x.shape[0]
    x_hi, x_lo = split(x)
    both = dot(jnp.concatenate([x_hi, x_lo], axis=0), hi, dims)
    return both[:rows] + (both[rows:] + dot(x_hi, lo, dims))


def fold(out):
    rows, cols = out.shape[0] // 2, out.shape[1] // 2
    return out[:rows, :cols] + (out[rows:, :cols] + out[:rows, cols:])


def stack(x):
    return jnp.concatenate(split(x), axis=0)


def pack(x):
    half = x.shape[0] // 2
    return jnp.concatenate([x[:half], x[half:]], axis=1)


def unpack(parts):
    n = parts[0].shape[1] // 2
    top = jnp.concatenate([p[:, :n] for p in parts], axis=1)
    return jnp.concatenate([top, jnp.concatenate([p[:, n:] for p in parts], axis=1)], axis=0)


def kernel(n_rows, n_cols, a_hbm, basis, cinv, gap, crhs, mask, m_out, p_out,
           stage, ahi, alo, bb, bt, chi, clo, whi, wlo, ghi, glo, v,
           nbb, nbgap, halo_in, am, dvec, grad, image, xs, dxs, e_s, nbc, vrecv, cm, nbcm, nbm, nbp,
           ebuf, pout0, pin0, pout, pin, amp_s, nbamps, xbuf, nbx, red,
           a_sem, bs, br, gs, gr, hs, hr, es, er, ps, pr, ams, amr, xss, xsr, cs, cr, ms, mr,
           vs, vr, ls, lr, qs, qr, rs, rr):
    row = lax.axis_index("row")
    col = lax.axis_index("col")
    me = row * n_cols + col
    n_dev = n_rows * n_cols
    m_len = ahi.shape[0]
    _, k, face = halo_in.shape
    mdev = nbb.shape[1]
    modes = n_cols * mdev
    width = red.shape[2]
    step_rows = m_len // a_sem.shape[0]
    n_blocks = a_sem.shape[0]
    has_nb = [row > 0, row < n_rows - 1, col > 0, col < n_cols - 1]
    outer = [jnp.logical_not(h) for h in has_nb]
    nbr = [(row - 1, col), (row + 1, col), (row, col - 1), (row, col + 1)]
    nb_outer = [[r == 0, r == n_rows - 1, c == 0, c == n_cols - 1] for r, c in nbr]
    cols_of = [slice(f * face, (f + 1) * face) for f in range(4)]

    def a_copy(i):
        rows = pl.ds(pl.multiple_of(i * step_rows, step_rows), step_rows)
        return pltpu.make_async_copy(a_hbm.at[0, 0, rows], stage.at[rows], a_sem.at[i])

    def a_start(i, carry):
        a_copy(i).start()
        return carry

    lax.fori_loop(0, n_blocks, a_start, 0)

    barrier = pltpu.get_barrier_semaphore()
    for d in range(1, n_dev):
        t = lax.rem(me + d, n_dev)
        pl.semaphore_signal(barrier, inc=1, device_id=(t // n_cols, lax.rem(t, n_cols)), device_id_type=MESH)
    pl.semaphore_wait(barrier, n_dev - 1)

    def remote(src, dst, ssem, rsem, where):
        return pltpu.make_async_remote_copy(
            src_ref=src, dst_ref=dst, send_sem=ssem, recv_sem=rsem, device_id=where, device_id_type=MESH)

    def face_start(f, src, dst, ssem, rsem):
        @pl.when(has_nb[f])
        def _():
            remote(src, dst.at[f ^ 1], ssem.at[f], rsem.at[f ^ 1], nbr[f]).start()

    def face_wait(f, src, dst, ssem, rsem):
        @pl.when(has_nb[f])
        def _():
            remote(src, dst.at[f], ssem.at[f], rsem.at[f], nbr[f]).wait()

    def outer_start(q, src, dst, ssem, rsem):
        for f in range(4):
            if f != q:
                @pl.when(jnp.logical_and(has_nb[f], outer[q]))
                def _():
                    remote(src(f, q), dst.at[f ^ 1, q], ssem.at[f, q], rsem.at[f ^ 1, q], nbr[f]).start()

    def outer_sent(q, src, dst, ssem, rsem):
        for f in range(4):
            if f != q:
                @pl.when(jnp.logical_and(has_nb[f], outer[q]))
                def _():
                    remote(src(f, q), dst.at[f ^ 1, q], ssem.at[f, q], rsem.at[f ^ 1, q], nbr[f]).wait_send()

    def on_outer_of_nb(do):
        for f in range(4):
            for q in range(4):
                if q != f ^ 1:
                    @pl.when(jnp.logical_and(has_nb[f], nb_outer[f][q]))
                    def _():
                        do(f, q)

    def outer_received(src, dst, ssem, rsem, do=None):
        def one(f, q):
            remote(src(f, q), dst.at[f, q], ssem.at[f, q], rsem.at[f, q], nbr[f]).wait_recv()
            if do is not None:
                do(f, q)
        on_outer_of_nb(one)

    def basis_face(f):
        return basis.at[0, 0, f]

    def gather_copies(use):
        return [remote(ebuf.at[use, row], ebuf.at[use, row], es.at[use, d], er.at[use, d], (lax.rem(row + d, n_rows), col))
                for d in range(1, n_rows)]

    def reduce_copies(use, src, dst):
        copies = []
        for d in range(1, n_cols):
            c = lax.rem(col + d, n_cols)
            copies.append(remote(src.at[c], dst.at[col], ps.at[use, d], pr.at[use, d], (row, c)))
        return copies

    def put_split(ref, x, f):
        hi, lo = split(x)
        ref[0:k, cols_of[f]] = hi
        ref[k:2 * k, cols_of[f]] = lo

    def apply_face(f):
        both = dot(xs[...], ahi[:, cols_of[f]], ((1,), (0,)))
        low = dot(xs[0:k, :], alo[:, cols_of[f]], ((1,), (0,)))
        return both[:k] + (both[k:] + low)

    def expand_face(every, f):
        mine = every[:, 0:mdev]
        theirs = every[:, (1 + f) * mdev:(2 + f) * mdev]
        hi, lo = split(jnp.concatenate([mine, theirs], axis=1))
        wide = jnp.concatenate([jnp.concatenate([hi, hi], axis=1), jnp.concatenate([lo, jnp.zeros_like(lo)], axis=1)], axis=0)
        both = dot(wide, bb[f], ((1,), (0,)))
        return both[:k] + both[k:]

    def restrict_face(x, f):
        return fold(dot(stack(x), bt[f], ((1,), (0,))))

    ebuf[0, row] = pack(crhs[0, 0])
    copies = gather_copies(0)
    for copy in copies:
        copy.start()
    for f in range(4):
        face_start(f, basis_face(f), nbb, bs, br)
    for f in range(4):
        contact = jnp.where(has_nb[f], 0, mask[0, 0, f:f + 1, :])
        cm[f] = jnp.where(contact == 1, 1.0, 0.0).astype(F32)
    for f in range(4):
        face_start(f, gap.at[0, 0, f], nbgap, gs, gr)
        face_start(f, cm, nbcm, ms, mr)
    zero_face = jnp.zeros((k, face), F32)
    zero_small = jnp.zeros((k // 2, 2 * mdev), F32)
    for f in range(4):
        @pl.when(outer[f])
        def _():
            nbb[f] = jnp.zeros((mdev, face), F32)
            nbgap[f] = zero_face
            halo_in[f] = zero_face
            nbamps[f] = zero_small
            nbx[f] = zero_small
    for c in range(n_cols):
        if c == 0:
            pout[c, 3] = zero_small
        if c == n_cols - 1:
            pout[c, 4] = zero_small

    def put_c(tile, at):
        hi, lo = split(tile.T)
        chi[:, at * modes:(at + 1) * modes] = hi
        clo[:, at * modes:(at + 1) * modes] = lo

    put_c(cinv[...], 0)
    for copy in copies:
        copy.wait()
    gathered = unpack([ebuf[0, r] for r in range(n_rows)])
    partial = dot3(gathered, chi[:, 0:modes], clo[:, 0:modes], ((1,), (0,)))
    for c in range(n_cols):
        pout0[c] = pack(partial[:, c * mdev:(c + 1) * mdev])
    copies = reduce_copies(0, pout0, pin0)
    for copy in copies:
        copy.start()
    pin0[col] = pout0[col]
    for f in range(4):
        face_wait(f, basis_face(f), nbb, bs, br)
        both = jnp.concatenate([basis[0, 0, f], nbb[f]], axis=0)
        hi, lo = split(both)
        bb[f, 0:2 * mdev] = hi
        bb[f, 2 * mdev:4 * mdev] = lo
        hi, lo = split(both.T)
        bt[f, :, 0:2 * mdev] = hi
        bt[f, :, 2 * mdev:4 * mdev] = lo
    for copy in copies:
        copy.wait()
    amps = pin0[0]
    for c in range(1, n_cols):
        amps = amps + pin0[c]
    amp_s[...] = amps
    for f in range(4):
        face_start(f, amp_s, nbamps, ams, amr)

    rd = jnp.zeros((k, mdev), F32)
    for f in range(4):
        face_wait(f, gap.at[0, 0, f], nbgap, gs, gr)
        face_wait(f, cm, nbcm, ms, mr)
        d = gap[0, 0, f] + nbgap[f]
        dvec[f] = d
        rd = rd + restrict_face(d, f)[:, 0:mdev]

    def a_split(i, carry):
        a_copy(i).wait()
        rows = pl.ds(pl.multiple_of(i * step_rows, step_rows), step_rows)
        hi, lo = split(stage[rows, :])
        ahi[rows, :] = hi
        alo[rows, :] = lo
        return carry

    lax.fori_loop(0, n_blocks, a_split, 0)
    for f in range(4):
        face_wait(f, amp_s, nbamps, ams, amr)
    for f in range(2):
        face_start(f, cinv, nbc, cs, cr)
    every = unpack([amp_s[...]] + [nbamps[f] for f in range(4)])

    for g in range(4):
        cols = cols_of[g]
        own = jnp.zeros((mdev, face), F32)
        for f in range(4):
            both = dot(bb[f], ahi[cols_of[f], cols], ((1,), (0,)))
            low = dot(bb[f, 0:2 * mdev], alo[cols_of[f], cols], ((1,), (0,)))
            both = both[:2 * mdev] + (both[2 * mdev:] + low)
            own = own + both[:mdev]
            stage[f * mdev:(f + 1) * mdev, cols] = both[mdev:]
            hi, lo = split(both[mdev:])
            whi[(f + 1) * mdev:(f + 2) * mdev, cols] = hi
            wlo[(f + 1) * mdev:(f + 2) * mdev, cols] = lo
        hi, lo = split(own)
        whi[0:mdev, cols] = hi
        wlo[0:mdev, cols] = lo

    def w_part(f, q):
        return stage.at[f * mdev:(f + 1) * mdev, cols_of[q]]

    for q in range(4):
        outer_start(q, w_part, vrecv, vs, vr)
    mine = jnp.zeros((5 * mdev, mdev), F32)
    theirs = []
    for f in range(4):
        w = jnp.concatenate([whi[:, cols_of[f]], wlo[:, cols_of[f]]], axis=0)
        part = fold(dot(w, bt[f], ((1,), (0,))))
        mine = mine + part[:, 0:mdev]
        theirs.append(part[:, mdev:])
    hi, lo = split(jnp.concatenate([mine] + theirs, axis=1))
    ghi[...] = hi
    glo[...] = lo

    def cross_start(w):
        for f in range(4):
            xbuf[f] = pack(w[:, (1 + f) * mdev:(2 + f) * mdev])
            face_start(f, xbuf.at[f], nbx, xss, xsr)

    def cross_end(w):
        for f in range(4):
            face_wait(f, xbuf.at[f], nbx, xss, xsr)
        total = (nbx[0] + nbx[1]) + (nbx[2] + nbx[3])
        half = k // 2
        return w[:, 0:mdev] + jnp.concatenate([total[:, :mdev], total[:, mdev:]], axis=0)

    u = dot3(every, ghi[...], glo[...], ((1,), (0,)))
    cross_start(u)
    def m_face(f, q):
        return m_out.at[0, 0, q]
    for f in range(4):
        m_out[0, 0, f] = expand_face(every, f)
        outer_start(f, m_face, nbm, ls, lr)
    for f in range(4):
        am[f] = dot3(every, whi[:, cols_of[f]], wlo[:, cols_of[f]], ((1,), (0,)))

    def put_v(f, q):
        hi, lo = split(vrecv[f, q])
        v[f, q, 0:mdev] = hi
        v[f, q, mdev:2 * mdev] = lo

    e_s[...] = cross_end(u) - rd
    for f in range(2):
        face_wait(f, cinv, nbc, cs, cr)
        @pl.when(has_nb[f])
        def _():
            put_c(nbc[f], 1 + f)
        @pl.when(outer[f])
        def _():
            chi[:, (1 + f) * modes:(2 + f) * modes] = jnp.zeros((chi.shape[0], modes), BF16)
            clo[:, (1 + f) * modes:(2 + f) * modes] = jnp.zeros((chi.shape[0], modes), BF16)
    outer_received(w_part, vrecv, vs, vr, put_v)
    outer_received(m_face, nbm, ls, lr)
    for q in range(4):
        outer_sent(q, w_part, vrecv, vs, vr)
        outer_sent(q, m_face, nbm, ls, lr)

    lane = lax.broadcasted_iota(jnp.int32, (k, width), 1)
    sub = lax.broadcasted_iota(jnp.int32, (k, width), 0)

    def p_face(f, q):
        return p_out.at[0, 0, q]

    def sum_copies():
        copies = []
        for d in range(1, n_dev):
            t = lax.rem(me + d, n_dev)
            copies.append(remote(red.at[me], red.at[me], rs.at[d], rr.at[d], (t // n_cols, lax.rem(t, n_cols))))
        return copies

    def iteration(step, ratio):
        ebuf[1, row] = pack(e_s[...])
        copies = gather_copies(1)
        for copy in copies:
            copy.start()

        @pl.when(step > 0)
        def _():
            for f in range(4):
                @pl.when(has_nb[f])
                def _():
                    m_out[0, 0, f] = m_out[0, 0, f] - ratio * p_out[0, 0, f]
                am[f] = am[f] - ratio * image[f]
            for f in range(4):
                @pl.when(outer[f])
                def _():
                    rows = cols_of[f]
                    change = dxs[:, rows]
                    for g in range(4):
                        both = dot(change, ahi[rows, cols_of[g]], ((1,), (0,)))
                        low = dot(change[0:k], alo[rows, cols_of[g]], ((1,), (0,)))
                        am[g] = am[g] + (both[:k] + (both[k:] + low))

        for f in range(4):
            face_start(f, am.at[f], halo_in, hs, hr)
        for copy in copies:
            copy.wait()
        gathered = unpack([ebuf[1, r] for r in range(n_rows)])
        partial = dot3(gathered, chi[...], clo[...], ((1,), (0,)))
        for c in range(n_cols):
            at = [c, n_cols + c, 2 * n_cols + c, c - 1 if c > 0 else None, c + 1 if c < n_cols - 1 else None]
            for i, j in enumerate(at):
                if j is not None:
                    pout[c, i] = pack(partial[:, j * mdev:(j + 1) * mdev])
        copies = reduce_copies(1, pout, pin)
        for copy in copies:
            copy.start()
        pin[col] = pout[col]
        squares = jnp.zeros((k, face), F32)
        for f in range(4):
            face_wait(f, am.at[f], halo_in, hs, hr)
            g = am[f] + halo_in[f] - dvec[f]
            grad[f] = g
            put_split(xs, g, f)
            weight = jnp.where(has_nb[f], 0.5, 1.0).astype(F32)
            squares = squares + weight * (g * g)
        numer = jnp.sum(squares, axis=1, keepdims=True)
        squares = jnp.zeros((k, face), F32)
        mine = jnp.zeros((k, mdev), F32)
        theirs = []
        for f in range(4):
            im = apply_face(f)
            image[f] = im
            squares = squares + grad[f] * im
            part = restrict_face(im, f)
            mine = mine + part[:, 0:mdev]
            theirs.append(part[:, mdev:])
        denom = jnp.sum(squares, axis=1, keepdims=True)
        wg = jnp.concatenate([mine] + theirs, axis=1)
        for copy in copies:
            copy.wait()
        total = pin[0]
        for c in range(1, n_cols):
            total = total + pin[c]
        every = unpack([total[i] for i in range(5)])
        wp = wg - dot3(every, ghi[...], glo[...], ((1,), (0,)))
        numer = numer - jnp.sum(e_s[...] * every[:, 0:mdev], axis=1, keepdims=True)
        denom = denom - jnp.sum(every * (wg + wp), axis=1, keepdims=True)
        packed = jnp.where(lane == sub, numer, 0.0) + jnp.where(lane == sub + k, denom, 0.0)
        red[me] = jnp.sum(packed, axis=0, keepdims=True)
        copies = sum_copies()
        for copy in copies:
            copy.start()
        cross_start(wp)
        for f in range(4):
            p_out[0, 0, f] = grad[f] - expand_face(every, f)
            outer_start(f, p_face, nbp, qs, qr)
        for f in range(4):
            image[f] = image[f] - dot3(every, whi[:, cols_of[f]], wlo[:, cols_of[f]], ((1,), (0,)))
        y = cross_end(wp)
        outer_received(p_face, nbp, qs, qr)
        for q in range(4):
            outer_sent(q, p_face, nbp, qs, qr)
        for copy in copies:
            copy.wait()
        total = jnp.sum(red[...], axis=0)
        numer_all = jnp.sum(jnp.where(lane == sub, total, 0.0), axis=1, keepdims=True)
        denom_all = jnp.sum(jnp.where(lane == sub + k, total, 0.0), axis=1, keepdims=True)
        ratio = numer_all / denom_all
        e_s[...] = e_s[...] - ratio * y

        def clamp(old, p, contact):
            linear = old - ratio * p
            new = jnp.where(contact > 0.5, jnp.maximum(linear, 0.0), linear)
            return new, new - linear

        for f in range(4):
            @pl.when(outer[f])
            def _():
                new, change = clamp(m_out[0, 0, f], p_out[0, 0, f], cm[f])
                m_out[0, 0, f] = new
                put_split(dxs, change, f)
                w = jnp.concatenate([whi[0:mdev, cols_of[f]], wlo[0:mdev, cols_of[f]]], axis=0)
                e_s[...] = e_s[...] + fold(dot(dxs[:, cols_of[f]], w, ((1,), (1,))))

        def nb_change(f, q):
            new, change = clamp(nbm[f, q], nbp[f, q], nbcm[f, q])
            nbm[f, q] = new
            e_s[...] = e_s[...] + fold(dot(stack(change), v[f, q], ((1,), (1,))))

        on_outer_of_nb(nb_change)
        return ratio

    ratio = lax.fori_loop(0, ITERS, iteration, jnp.zeros((k, 1), F32))
    for f in range(4):
        @pl.when(has_nb[f])
        def _():
            m_out[0, 0, f] = m_out[0, 0, f] - ratio * p_out[0, 0, f]


def solution(mesh):
    n_rows, n_cols = mesh.shape["row"], mesh.shape["col"]

    def shards(dual_ops, basis, coarse_inverse, gap_rhs, coarse_rhs, contact_mask):
        m_len = dual_ops.shape[-1]
        _, _, _, k, face = gap_rhs.shape
        mdev = basis.shape[3]
        width = -(-2 * k // 128) * 128
        blocks = math.gcd(m_len, 32)
        n_dev = n_rows * n_cols
        vm = pltpu.VMEM
        dma = pltpu.SemaphoreType.DMA
        small = (k // 2, 2 * mdev)
        c_rows, c_cols = coarse_inverse.shape
        faces = vm((4, k, face), F32)
        out = jax.ShapeDtypeStruct(gap_rhs.shape, F32)
        in_vmem = pl.BlockSpec(memory_space=pltpu.VMEM)
        return pl.pallas_call(
            functools.partial(kernel, n_rows, n_cols),
            out_shape=(out, out),
            in_specs=[pl.BlockSpec(memory_space=pl.ANY)] + [in_vmem] * 5,
            out_specs=(in_vmem, in_vmem),
            scratch_shapes=[
                vm((m_len, m_len), F32), vm((m_len, m_len), BF16), vm((m_len, m_len), BF16),
                vm((4, 4 * mdev, face), BF16), vm((4, face, 4 * mdev), BF16),
                vm((c_cols, 3 * c_rows), BF16), vm((c_cols, 3 * c_rows), BF16),
                vm((5 * mdev, m_len), BF16), vm((5 * mdev, m_len), BF16),
                vm((5 * mdev, 5 * mdev), BF16), vm((5 * mdev, 5 * mdev), BF16),
                vm((4, 4, 2 * mdev, face), BF16),
                vm((4, mdev, face), F32), faces, faces, faces, faces, faces, faces,
                vm((2 * k, m_len), BF16), vm((2 * k, m_len), BF16), vm((k, mdev), F32),
                vm((2, c_rows, c_cols), F32), vm((4, 4, mdev, face), F32),
                vm((4, 1, face), F32), vm((4, 4, 1, face), F32), vm((4, 4, k, face), F32), vm((4, 4, k, face), F32),
                vm((2, n_rows, *small), F32), vm((n_cols, *small), F32), vm((n_cols, *small), F32),
                vm((n_cols, 5, *small), F32), vm((n_cols, 5, *small), F32),
                vm(small, F32), vm((4, *small), F32), vm((4, *small), F32), vm((4, *small), F32),
                vm((n_dev, 1, width), F32),
                dma((blocks,)),
                dma((4,)), dma((4,)), dma((4,)), dma((4,)), dma((4,)), dma((4,)),
                dma((2, n_rows)), dma((2, n_rows)), dma((2, n_cols)), dma((2, n_cols)),
                dma((4,)), dma((4,)), dma((4,)), dma((4,)), dma((2,)), dma((2,)), dma((4,)), dma((4,)),
                dma((4, 4)), dma((4, 4)), dma((4, 4)), dma((4, 4)), dma((4, 4)), dma((4, 4)),
                dma((n_dev,)), dma((n_dev,)),
            ],
            compiler_params=pltpu.CompilerParams(
                collective_id=0, has_side_effects=True, vmem_limit_bytes=62 * 1024 * 1024),
        )(dual_ops, basis, coarse_inverse, gap_rhs, coarse_rhs, contact_mask)

    return jax.shard_map(
        shards,
        mesh=mesh,
        in_specs=(
            P("row", "col", None, None),
            P("row", "col", None, None, None),
            P("row", "col"),
            P("row", "col", None, None, None),
            P("row", "col", None, None),
            P("row", "col", None, None),
        ),
        out_specs=(P("row", "col", None, None, None), P("row", "col", None, None, None)),
        check_vma=False,
    )
```

```python
import functools
import math

import jax
import jax.numpy as jnp
from jax import lax
from jax.experimental import pallas as pl
from jax.experimental.pallas import tpu as pltpu
from jax.sharding import PartitionSpec as P

ITERS = 6
MESH = pl.DeviceIdType.MESH
F32 = jnp.float32
BF16 = jnp.bfloat16


def split(x):
    hi = x.astype(BF16)
    return hi, (x - hi.astype(F32)).astype(BF16)


def dot(a, b, dims):
    return lax.dot_general(a, b, (dims, ((), ())), preferred_element_type=F32)


def dot3(x, hi, lo, dims):
    rows = x.shape[0]
    x_hi, x_lo = split(x)
    both = dot(jnp.concatenate([x_hi, x_lo], axis=0), hi, dims)
    return both[:rows] + (both[rows:] + dot(x_hi, lo, dims))


def fold(out):
    rows, cols = out.shape[0] // 2, out.shape[1] // 2
    return out[:rows, :cols] + (out[rows:, :cols] + out[:rows, cols:])


def stack(x):
    return jnp.concatenate(split(x), axis=0)


def pack(x):
    half = x.shape[0] // 2
    return jnp.concatenate([x[:half], x[half:]], axis=1)


def unpack(parts):
    n = parts[0].shape[1] // 2
    top = jnp.concatenate([p[:, :n] for p in parts], axis=1)
    return jnp.concatenate([top, jnp.concatenate([p[:, n:] for p in parts], axis=1)], axis=0)


def kernel(n_rows, n_cols, a_hbm, basis_hbm, cinv_hbm, gap_hbm, crhs_hbm, mask_hbm, m_hbm, p_hbm,
           basis, cinv, gap, crhs, mask, m_out, p_out,
           stage, ahi, alo, bb, bt, chi, clo, whi, wlo, ghi, glo, v,
           nbb, nbgap, halo_in, am, dvec, grad, image, xs, dxs, e_s, nbc, vrecv, cm, nbcm, nbm, nbp,
           ebuf, pout0, pin0, pout, pin, amp_s, nbamps, xbuf, nbx, red, tot,
           in_sem, out_sem, a_sem, bs, br, gs, gr, hs, hr, es, er, ps, pr, ams, amr, xss, xsr, cs, cr, ms, mr,
           vs, vr, ls, lr, qs, qr, rs, rr):
    row = lax.axis_index("row")
    col = lax.axis_index("col")
    me = row * n_cols + col
    n_dev = n_rows * n_cols
    m_len = ahi.shape[0]
    _, k, face = halo_in.shape
    mdev = nbb.shape[1]
    modes = n_cols * mdev
    width = red.shape[2]
    step_rows = m_len // a_sem.shape[0]
    n_blocks = a_sem.shape[0]
    has_nb = [row > 0, row < n_rows - 1, col > 0, col < n_cols - 1]
    outer = [jnp.logical_not(h) for h in has_nb]
    nbr = [(row - 1, col), (row + 1, col), (row, col - 1), (row, col + 1)]
    nb_outer = [[r == 0, r == n_rows - 1, c == 0, c == n_cols - 1] for r, c in nbr]
    cols_of = [slice(f * face, (f + 1) * face) for f in range(4)]

    def a_copy(i):
        rows = pl.ds(pl.multiple_of(i * step_rows, step_rows), step_rows)
        return pltpu.make_async_copy(a_hbm.at[0, 0, rows], stage.at[rows], a_sem.at[i])

    def a_start(i, carry):
        a_copy(i).start()
        return carry

    loads = [pltpu.make_async_copy(src.at[0, 0], dst, in_sem.at[i]) for i, (src, dst) in enumerate(
        [(crhs_hbm, crhs), (basis_hbm, basis), (mask_hbm, mask), (gap_hbm, gap)])]
    loads.insert(1, pltpu.make_async_copy(cinv_hbm, cinv, in_sem.at[4]))
    for load in loads:
        load.start()
    lax.fori_loop(0, n_blocks, a_start, 0)

    barrier = pltpu.get_barrier_semaphore()
    others = [jnp.where(me + d < n_dev, me + d, me + d - n_dev) for d in range(1, n_dev)]
    for t in others:
        pl.semaphore_signal(barrier, inc=1, device_id=t, device_id_type=pl.DeviceIdType.LOGICAL)

    def remote(src, dst, ssem, rsem, where):
        return pltpu.make_async_remote_copy(
            src_ref=src, dst_ref=dst, send_sem=ssem, recv_sem=rsem, device_id=where, device_id_type=MESH)

    def face_start(f, src, dst, ssem, rsem):
        @pl.when(has_nb[f])
        def _():
            remote(src, dst.at[f ^ 1], ssem.at[f], rsem.at[f ^ 1], nbr[f]).start()

    def face_wait(f, src, dst, ssem, rsem):
        @pl.when(has_nb[f])
        def _():
            remote(src, dst.at[f], ssem.at[f], rsem.at[f], nbr[f]).wait()

    def outer_start(q, src, dst, ssem, rsem):
        for f in range(4):
            if f != q:
                @pl.when(jnp.logical_and(has_nb[f], outer[q]))
                def _():
                    remote(src(f, q), dst.at[f ^ 1, q], ssem.at[f, q], rsem.at[f ^ 1, q], nbr[f]).start()

    def outer_sent(q, src, dst, ssem, rsem):
        for f in range(4):
            if f != q:
                @pl.when(jnp.logical_and(has_nb[f], outer[q]))
                def _():
                    remote(src(f, q), dst.at[f ^ 1, q], ssem.at[f, q], rsem.at[f ^ 1, q], nbr[f]).wait_send()

    def on_outer_of_nb(do):
        for f in range(4):
            for q in range(4):
                if q != f ^ 1:
                    @pl.when(jnp.logical_and(has_nb[f], nb_outer[f][q]))
                    def _():
                        do(f, q)

    def outer_received(src, dst, ssem, rsem, do=None):
        def one(f, q):
            remote(src(f, q), dst.at[f, q], ssem.at[f, q], rsem.at[f, q], nbr[f]).wait_recv()
            if do is not None:
                do(f, q)
        on_outer_of_nb(one)

    def basis_face(f):
        return basis.at[f]

    def gather_copies(use):
        return [remote(ebuf.at[use, row], ebuf.at[use, row], es.at[use], er.at[use], (lax.rem(row + d, n_rows), col))
                for d in range(1, n_rows)]

    def gather_wait(use):
        part = ebuf.at[use, pl.ds(0, n_rows - 1)]
        remote(part, part, es.at[use], er.at[use], (lax.rem(row + 1, n_rows), col)).wait()

    def tile_copy(f, slot, half):
        rows = pl.ds(half * (cinv.shape[0] // 2), cinv.shape[0] // 2)
        return remote(cinv.at[rows], nbc.at[slot, rows], cs.at[f, half], cr.at[slot, half], nbr[f])

    def tile_start(half):
        for f in range(2):
            @pl.when(has_nb[f])
            def _():
                tile_copy(f, f ^ 1, half).start()

    def reduce_wait(use, src, dst):
        part = pl.ds(0, n_cols - 1)
        remote(src.at[part], dst.at[part], ps.at[use], pr.at[use], (row, lax.rem(col + 1, n_cols))).wait()

    def reduce_copies(use, src, dst):
        copies = []
        for d in range(1, n_cols):
            c = lax.rem(col + d, n_cols)
            copies.append(remote(src.at[c], dst.at[col], ps.at[use], pr.at[use], (row, c)))
        return copies

    def put_split(ref, x, f):
        hi, lo = split(x)
        ref[0:k, cols_of[f]] = hi
        ref[k:2 * k, cols_of[f]] = lo

    def apply_face(f):
        both = dot(xs[...], ahi[:, cols_of[f]], ((1,), (0,)))
        low = dot(xs[0:k, :], alo[:, cols_of[f]], ((1,), (0,)))
        return both[:k] + (both[k:] + low)

    def expand_face(every, f):
        mine = every[:, 0:mdev]
        theirs = every[:, (1 + f) * mdev:(2 + f) * mdev]
        hi, lo = split(jnp.concatenate([mine, theirs], axis=1))
        wide = jnp.concatenate([jnp.concatenate([hi, hi], axis=1), jnp.concatenate([lo, jnp.zeros_like(lo)], axis=1)], axis=0)
        both = dot(wide, bb[f], ((1,), (0,)))
        return both[:k] + both[k:]

    def restrict_face(x, f):
        return fold(dot(stack(x), bt[f], ((1,), (0,))))

    def a_split(i, carry):
        a_copy(i).wait()
        rows = pl.ds(pl.multiple_of(i * step_rows, step_rows), step_rows)
        hi, lo = split(stage[rows, :])
        ahi[rows, :] = hi
        alo[rows, :] = lo
        return carry

    def put_c(tile, at):
        hi, lo = split(tile.T)
        chi[:, at * modes:(at + 1) * modes] = hi
        clo[:, at * modes:(at + 1) * modes] = lo

    zero_face = jnp.zeros((k, face), F32)
    zero_small = jnp.zeros((k // 2, 2 * mdev), F32)
    for f in range(4):
        @pl.when(outer[f])
        def _():
            nbb[f] = jnp.zeros((mdev, face), F32)
            nbgap[f] = zero_face
            halo_in[f] = zero_face
            nbamps[f] = zero_small
            nbx[f] = zero_small
    pout[0, 3] = zero_small
    pout[n_cols - 1, 4] = zero_small
    chi[:, modes:] = jnp.zeros((chi.shape[0], 2 * modes), BF16)
    clo[:, modes:] = jnp.zeros((chi.shape[0], 2 * modes), BF16)
    for load in loads:
        load.wait()
    ebuf[0, row] = pack(crhs[...])
    for f in range(4):
        contact = jnp.where(has_nb[f], 0, mask[f:f + 1, :])
        cm[f] = jnp.where(contact == 1, 1.0, 0.0).astype(F32)
    put_c(cinv[...], 0)
    early = n_blocks // 4
    lax.fori_loop(0, early, a_split, 0)
    pl.semaphore_wait(barrier, n_dev - 1)

    gathers = gather_copies(0)
    for copy in gathers:
        copy.start()
    for f in range(4):
        face_start(f, basis_face(f), nbb, bs, br)
    lax.fori_loop(early, n_blocks, a_split, 0)
    gather_wait(0)
    gathered = unpack([ebuf[0, r] for r in range(n_rows)])
    partial = dot3(gathered, chi[:, 0:modes], clo[:, 0:modes], ((1,), (0,)))
    for c in range(n_cols):
        pout0[c] = pack(partial[:, c * mdev:(c + 1) * mdev])
    reduces = reduce_copies(0, pout0, pin0)
    for copy in reduces:
        copy.start()
    pin0[col] = pout0[col]
    for f in range(4):
        face_start(f, gap.at[f], nbgap, gs, gr)
        face_start(f, cm, nbcm, ms, mr)
    for f in range(4):
        face_wait(f, basis_face(f), nbb, bs, br)
        both = jnp.concatenate([basis[f], nbb[f]], axis=0)
        hi, lo = split(both)
        bb[f, 0:2 * mdev] = hi
        bb[f, 2 * mdev:4 * mdev] = lo
        hi, lo = split(both.T)
        bt[f, :, 0:2 * mdev] = hi
        bt[f, :, 2 * mdev:4 * mdev] = lo

    def w_cols(g):
        cols = cols_of[g]
        own = jnp.zeros((mdev, face), F32)
        for f in range(4):
            both = dot(bb[f], ahi[cols_of[f], cols], ((1,), (0,)))
            low = dot(bb[f, 0:2 * mdev], alo[cols_of[f], cols], ((1,), (0,)))
            both = both[:2 * mdev] + (both[2 * mdev:] + low)
            own = own + both[:mdev]
            stage[f * mdev:(f + 1) * mdev, cols] = both[mdev:]
            hi, lo = split(both[mdev:])
            whi[(f + 1) * mdev:(f + 2) * mdev, cols] = hi
            wlo[(f + 1) * mdev:(f + 2) * mdev, cols] = lo
        hi, lo = split(own)
        whi[0:mdev, cols] = hi
        wlo[0:mdev, cols] = lo

    w_cols(0)
    w_cols(1)
    reduce_wait(0, pout0, pin0)
    amps = pin0[0]
    for c in range(1, n_cols):
        amps = amps + pin0[c]
    amp_s[...] = amps
    for f in range(4):
        face_start(f, amp_s, nbamps, ams, amr)
    w_cols(2)
    w_cols(3)

    def w_part(f, q):
        return stage.at[f * mdev:(f + 1) * mdev, cols_of[q]]

    mine = jnp.zeros((5 * mdev, mdev), F32)
    theirs = []
    for f in range(4):
        w = jnp.concatenate([whi[:, cols_of[f]], wlo[:, cols_of[f]]], axis=0)
        part = fold(dot(w, bt[f], ((1,), (0,))))
        mine = mine + part[:, 0:mdev]
        theirs.append(part[:, mdev:])
    hi, lo = split(jnp.concatenate([mine] + theirs, axis=1))
    ghi[...] = hi
    glo[...] = lo

    def cross_start(w):
        for f in range(4):
            xbuf[f] = pack(w[:, (1 + f) * mdev:(2 + f) * mdev])
            face_start(f, xbuf.at[f], nbx, xss, xsr)

    def cross_end(w):
        for f in range(4):
            face_wait(f, xbuf.at[f], nbx, xss, xsr)
        total = (nbx[0] + nbx[1]) + (nbx[2] + nbx[3])
        return w[:, 0:mdev] + jnp.concatenate([total[:, :mdev], total[:, mdev:]], axis=0)

    for f in range(4):
        face_wait(f, amp_s, nbamps, ams, amr)
    every = unpack([amp_s[...]] + [nbamps[f] for f in range(4)])
    u = dot3(every, ghi[...], glo[...], ((1,), (0,)))
    cross_start(u)

    def m_face(f, q):
        return m_out.at[q]

    rd = jnp.zeros((k, mdev), F32)
    for f in range(4):
        face_wait(f, gap.at[f], nbgap, gs, gr)
        face_wait(f, cm, nbcm, ms, mr)
        d = gap[f] + nbgap[f]
        dvec[f] = d
        rd = rd + restrict_face(d, f)[:, 0:mdev]
    for f in range(4):
        am[f] = dot3(every, whi[:, cols_of[f]], wlo[:, cols_of[f]], ((1,), (0,)))
    def gather_start():
        ebuf[1, row] = pack(e_s[...])
        for copy in gather_copies(1):
            copy.start()

    e_s[...] = cross_end(u) - rd
    gather_start()
    for f in range(4):
        m_out[f] = expand_face(every, f)

    def put_v(f, q):
        hi, lo = split(vrecv[f, q])
        v[f, q, 0:mdev] = hi
        v[f, q, mdev:2 * mdev] = lo

    lane = lax.broadcasted_iota(jnp.int32, (k, width), 1)
    sub = lax.broadcasted_iota(jnp.int32, (k, width), 0)

    def p_face(f, q):
        return p_out.at[q]

    def sum_copy(src, dst, t):
        return pltpu.make_async_remote_copy(
            src_ref=src, dst_ref=dst, send_sem=rs.at[0], recv_sem=rr.at[0], device_id=t,
            device_id_type=pl.DeviceIdType.LOGICAL)

    sums = sum_copy(red.at[pl.ds(0, n_dev - 1)], red.at[pl.ds(0, n_dev - 1)], others[0])

    p_store = pltpu.make_async_copy(p_out, p_hbm.at[0, 0], out_sem.at[0])

    def iteration(step, ratio):
        @pl.when(step > 0)
        def _():
            for f in range(4):
                @pl.when(has_nb[f])
                def _():
                    m_out[f] = m_out[f] - ratio * p_out[f]
                am[f] = am[f] - ratio * image[f]
            for f in range(4):
                @pl.when(outer[f])
                def _():
                    rows = cols_of[f]
                    change = dxs[:, rows]
                    for g in range(4):
                        both = dot(change, ahi[rows, cols_of[g]], ((1,), (0,)))
                        low = dot(change[0:k], alo[rows, cols_of[g]], ((1,), (0,)))
                        am[g] = am[g] + (both[:k] + (both[k:] + low))

        for f in range(4):
            face_start(f, am.at[f], halo_in, hs, hr)
        gather_wait(1)
        gathered = unpack([ebuf[1, r] for r in range(n_rows)])
        partial = dot3(gathered, chi[...], clo[...], ((1,), (0,)))
        for c in range(n_cols):
            at = [c, n_cols + c, 2 * n_cols + c, c - 1 if c > 0 else None, c + 1 if c < n_cols - 1 else None]
            for i, j in enumerate(at):
                if j is not None:
                    pout[c, i] = pack(partial[:, j * mdev:(j + 1) * mdev])
        copies = reduce_copies(1, pout, pin)
        for copy in copies:
            copy.start()
        pin[col] = pout[col]

        @pl.when(step == 0)
        def _():
            for q in range(4):
                outer_start(q, w_part, vrecv, vs, vr)
                outer_start(q, m_face, nbm, ls, lr)

        @pl.when(step == 1)
        def _():
            tile_start(0)

        @pl.when(step == 2)
        def _():
            tile_start(1)

        squares = jnp.zeros((k, face), F32)
        for f in range(4):
            face_wait(f, am.at[f], halo_in, hs, hr)
            g = am[f] + halo_in[f] - dvec[f]
            grad[f] = g
            put_split(xs, g, f)
            weight = jnp.where(has_nb[f], 0.5, 1.0).astype(F32)
            squares = squares + weight * (g * g)
        numer = jnp.sum(squares, axis=1, keepdims=True)
        squares = jnp.zeros((k, face), F32)
        mine = jnp.zeros((k, mdev), F32)
        theirs = []
        for f in range(4):
            im = apply_face(f)
            image[f] = im
            squares = squares + grad[f] * im
            part = restrict_face(im, f)
            mine = mine + part[:, 0:mdev]
            theirs.append(part[:, mdev:])
        denom = jnp.sum(squares, axis=1, keepdims=True)
        wg = jnp.concatenate([mine] + theirs, axis=1)
        reduce_wait(1, pout, pin)
        total = pin[0]
        for c in range(1, n_cols):
            total = total + pin[c]
        tot[...] = total

        @pl.when(step <= 2)
        def _():
            amp_s[...] = tot[0]
            for f in range(2):
                face_start(f, amp_s, nbamps, ams, amr)
            for f in range(2):
                face_wait(f, amp_s, nbamps, ams, amr)
                tot[1 + f] = nbamps[f]

        every = unpack([tot[i] for i in range(5)])
        wp = wg - dot3(every, ghi[...], glo[...], ((1,), (0,)))
        numer = numer - jnp.sum(e_s[...] * every[:, 0:mdev], axis=1, keepdims=True)
        denom = denom - jnp.sum(every * (wg + wp), axis=1, keepdims=True)
        packed = jnp.where(lane == sub, numer, 0.0) + jnp.where(lane == sub + k, denom, 0.0)
        red[me] = jnp.sum(packed, axis=0, keepdims=True)
        for t in others:
            sum_copy(red.at[me], red.at[me], t).start()
        cross_start(wp)
        for f in range(4):
            p_out[f] = grad[f] - expand_face(every, f)
            outer_start(f, p_face, nbp, qs, qr)
        for f in range(4):
            image[f] = image[f] - dot3(every, whi[:, cols_of[f]], wlo[:, cols_of[f]], ((1,), (0,)))
        @pl.when(step == 0)
        def _():
            outer_received(w_part, vrecv, vs, vr, put_v)
            outer_received(m_face, nbm, ls, lr)
            for q in range(4):
                outer_sent(q, w_part, vrecv, vs, vr)
                outer_sent(q, m_face, nbm, ls, lr)

        @pl.when(step == 2)
        def _():
            for f in range(2):
                @pl.when(has_nb[f])
                def _():
                    for half in range(2):
                        tile_copy(f, f, half).wait()
                    put_c(nbc[f], 1 + f)

        @pl.when(step == ITERS - 1)
        def _():
            p_store.start()

        y = cross_end(wp)
        outer_received(p_face, nbp, qs, qr)
        for q in range(4):
            outer_sent(q, p_face, nbp, qs, qr)
        sums.wait()
        total = jnp.sum(red[...], axis=0)
        numer_all = jnp.sum(jnp.where(lane == sub, total, 0.0), axis=1, keepdims=True)
        denom_all = jnp.sum(jnp.where(lane == sub + k, total, 0.0), axis=1, keepdims=True)
        ratio = numer_all / denom_all
        e_s[...] = e_s[...] - ratio * y

        def clamp(old, p, contact):
            linear = old - ratio * p
            new = jnp.where(contact > 0.5, jnp.maximum(linear, 0.0), linear)
            return new, new - linear

        for f in range(4):
            @pl.when(outer[f])
            def _():
                new, change = clamp(m_out[f], p_out[f], cm[f])
                m_out[f] = new
                put_split(dxs, change, f)
                w = jnp.concatenate([whi[0:mdev, cols_of[f]], wlo[0:mdev, cols_of[f]]], axis=0)
                e_s[...] = e_s[...] + fold(dot(dxs[:, cols_of[f]], w, ((1,), (1,))))

        def nb_change(f, q):
            new, change = clamp(nbm[f, q], nbp[f, q], nbcm[f, q])
            nbm[f, q] = new
            e_s[...] = e_s[...] + fold(dot(stack(change), v[f, q], ((1,), (1,))))

        on_outer_of_nb(nb_change)

        @pl.when(step < ITERS - 1)
        def _():
            gather_start()

        return ratio

    ratio = lax.fori_loop(0, ITERS, iteration, jnp.zeros((k, 1), F32))
    for f in range(4):
        @pl.when(has_nb[f])
        def _():
            m_out[f] = m_out[f] - ratio * p_out[f]
    m_store = pltpu.make_async_copy(m_out, m_hbm.at[0, 0], out_sem.at[1])
    m_store.start()
    p_store.wait()
    m_store.wait()


def hand_on(m_in, p_in, m_out, p_out):
    m_out[...] = m_in[...]
    p_out[...] = p_in[...]


def solution(mesh):
    n_rows, n_cols = mesh.shape["row"], mesh.shape["col"]

    def shards(dual_ops, basis, coarse_inverse, gap_rhs, coarse_rhs, contact_mask):
        m_len = dual_ops.shape[-1]
        _, _, _, k, face = gap_rhs.shape
        mdev = basis.shape[3]
        width = -(-2 * k // 128) * 128
        blocks = math.gcd(m_len, 32)
        n_dev = n_rows * n_cols
        vm = pltpu.VMEM
        dma = pltpu.SemaphoreType.DMA
        small = (k // 2, 2 * mdev)
        c_rows, c_cols = coarse_inverse.shape
        faces = vm((4, k, face), F32)
        out = jax.ShapeDtypeStruct(gap_rhs.shape, F32)
        anywhere = pl.BlockSpec(memory_space=pl.ANY)
        results = pl.pallas_call(
            functools.partial(kernel, n_rows, n_cols),
            out_shape=(out, out),
            in_specs=[anywhere] * 6,
            out_specs=(anywhere, anywhere),
            scratch_shapes=[
                vm((4, mdev, face), F32), vm(coarse_inverse.shape, F32), faces, vm((k, mdev), F32), vm((4, face), jnp.int32),
                faces, faces,
                vm((m_len, m_len), F32), vm((m_len, m_len), BF16), vm((m_len, m_len), BF16),
                vm((4, 4 * mdev, face), BF16), vm((4, face, 4 * mdev), BF16),
                vm((c_cols, 3 * c_rows), BF16), vm((c_cols, 3 * c_rows), BF16),
                vm((5 * mdev, m_len), BF16), vm((5 * mdev, m_len), BF16),
                vm((5 * mdev, 5 * mdev), BF16), vm((5 * mdev, 5 * mdev), BF16),
                vm((4, 4, 2 * mdev, face), BF16),
                vm((4, mdev, face), F32), faces, faces, faces, faces, faces, faces,
                vm((2 * k, m_len), BF16), vm((2 * k, m_len), BF16), vm((k, mdev), F32),
                vm((2, c_rows, c_cols), F32), vm((4, 4, mdev, face), F32),
                vm((4, 1, face), F32), vm((4, 4, 1, face), F32), vm((4, 4, k, face), F32), vm((4, 4, k, face), F32),
                vm((2, n_rows, *small), F32), vm((n_cols, *small), F32), vm((n_cols, *small), F32),
                vm((n_cols, 5, *small), F32), vm((n_cols, 5, *small), F32),
                vm(small, F32), vm((4, *small), F32), vm((4, *small), F32), vm((4, *small), F32),
                vm((n_dev, 1, width), F32), vm((5, *small), F32),
                dma((5,)), dma((2,)), dma((blocks,)),
                dma((4,)), dma((4,)), dma((4,)), dma((4,)), dma((4,)), dma((4,)),
                dma((2,)), dma((2,)), dma((2,)), dma((2,)),
                dma((4,)), dma((4,)), dma((4,)), dma((4,)), dma((2, 2)), dma((2, 2)), dma((4,)), dma((4,)),
                dma((4, 4)), dma((4, 4)), dma((4, 4)), dma((4, 4)), dma((4, 4)), dma((4, 4)),
                dma((1,)), dma((1,)),
            ],
            compiler_params=pltpu.CompilerParams(
                collective_id=0, has_side_effects=True, vmem_limit_bytes=62 * 1024 * 1024),
        )(dual_ops, basis, coarse_inverse, gap_rhs, coarse_rhs, contact_mask)
        in_vmem = pl.BlockSpec(memory_space=pltpu.VMEM)
        return pl.pallas_call(
            hand_on, out_shape=(out, out), in_specs=[in_vmem] * 2, out_specs=(in_vmem, in_vmem))(*results)

    return jax.shard_map(
        shards,
        mesh=mesh,
        in_specs=(
            P("row", "col", None, None),
            P("row", "col", None, None, None),
            P("row", "col"),
            P("row", "col", None, None, None),
            P("row", "col", None, None),
            P("row", "col", None, None),
        ),
        out_specs=(P("row", "col", None, None, None), P("row", "col", None, None, None)),
        check_vma=False,
    )
```

```python
import functools
import math

import jax
import jax.numpy as jnp
from jax import lax
from jax.experimental import pallas as pl
from jax.experimental.pallas import tpu as pltpu
from jax.sharding import PartitionSpec as P

ITERS = 6
MESH = pl.DeviceIdType.MESH
F32 = jnp.float32
BF16 = jnp.bfloat16


def split(x):
    hi = x.astype(BF16)
    return hi, (x - hi.astype(F32)).astype(BF16)


def dot(a, b, dims):
    return lax.dot_general(a, b, (dims, ((), ())), preferred_element_type=F32)


def dot3(x, hi, lo, dims):
    rows = x.shape[0]
    x_hi, x_lo = split(x)
    both = dot(jnp.concatenate([x_hi, x_lo], axis=0), hi, dims)
    return both[:rows] + (both[rows:] + dot(x_hi, lo, dims))


def fold(out):
    rows, cols = out.shape[0] // 2, out.shape[1] // 2
    return out[:rows, :cols] + (out[rows:, :cols] + out[:rows, cols:])


def stack(x):
    return jnp.concatenate(split(x), axis=0)


def pack(x):
    half = x.shape[0] // 2
    return jnp.concatenate([x[:half], x[half:]], axis=1)


def unpack(parts):
    n = parts[0].shape[1] // 2
    top = jnp.concatenate([p[:, :n] for p in parts], axis=1)
    return jnp.concatenate([top, jnp.concatenate([p[:, n:] for p in parts], axis=1)], axis=0)


def kernel(n_rows, n_cols, a_hbm, basis_hbm, cinv_hbm, gap_hbm, crhs_hbm, mask_hbm, m_hbm, p_hbm,
           basis, cinv, gap, crhs, mask, m_out, p_out,
           stage, ahi, alo, bb, bt, chi, clo, whi, wlo, ghi, glo, v,
           nbb, nbgap, halo_in, am, dvec, grad, image, xs, dxs, e_s, nbc, vrecv, cm, nbcm, nbm, nbp,
           ebuf, pout0, pin0, pout, pin, amp_s, nbamps, xbuf, nbx, red, tot,
           in_sem, out_sem, a_sem, bs, br, gs, gr, hs, hr, es, er, ps, pr, ams, amr, xss, xsr, cs, cr, ms, mr,
           vs, vr, ls, lr, qs, qr, rs, rr):
    row = lax.axis_index("row")
    col = lax.axis_index("col")
    me = row * n_cols + col
    n_dev = n_rows * n_cols
    m_len = ahi.shape[0]
    _, k, face = halo_in.shape
    mdev = nbb.shape[1]
    modes = n_cols * mdev
    width = red.shape[2]
    step_rows = m_len // a_sem.shape[0]
    n_blocks = a_sem.shape[0]
    has_nb = [row > 0, row < n_rows - 1, col > 0, col < n_cols - 1]
    outer = [jnp.logical_not(h) for h in has_nb]
    nbr = [(row - 1, col), (row + 1, col), (row, col - 1), (row, col + 1)]
    nb_outer = [[r == 0, r == n_rows - 1, c == 0, c == n_cols - 1] for r, c in nbr]
    cols_of = [slice(f * face, (f + 1) * face) for f in range(4)]

    def a_copy(i):
        rows = pl.ds(pl.multiple_of(i * step_rows, step_rows), step_rows)
        return pltpu.make_async_copy(a_hbm.at[0, 0, rows], stage.at[rows], a_sem.at[i])

    def a_start(i, carry):
        a_copy(i).start()
        return carry

    loads = [pltpu.make_async_copy(src.at[0, 0], dst, in_sem.at[i]) for i, (src, dst) in enumerate(
        [(crhs_hbm, crhs), (basis_hbm, basis), (mask_hbm, mask), (gap_hbm, gap)])]
    loads.insert(1, pltpu.make_async_copy(cinv_hbm, cinv, in_sem.at[4]))
    for load in loads:
        load.start()
    lax.fori_loop(0, n_blocks, a_start, 0)

    barrier = pltpu.get_barrier_semaphore()
    others = [jnp.where(me + d < n_dev, me + d, me + d - n_dev) for d in range(1, n_dev)]
    for t in others:
        pl.semaphore_signal(barrier, inc=1, device_id=t, device_id_type=pl.DeviceIdType.LOGICAL)

    def remote(src, dst, ssem, rsem, where):
        return pltpu.make_async_remote_copy(
            src_ref=src, dst_ref=dst, send_sem=ssem, recv_sem=rsem, device_id=where, device_id_type=MESH)

    def face_start(f, src, dst, ssem, rsem):
        @pl.when(has_nb[f])
        def _():
            remote(src, dst.at[f ^ 1], ssem.at[f], rsem.at[f ^ 1], nbr[f]).start()

    def face_wait(f, src, dst, ssem, rsem):
        @pl.when(has_nb[f])
        def _():
            remote(src, dst.at[f], ssem.at[f], rsem.at[f], nbr[f]).wait()

    def outer_start(q, src, dst, ssem, rsem):
        for f in range(4):
            if f != q:
                @pl.when(jnp.logical_and(has_nb[f], outer[q]))
                def _():
                    remote(src(f, q), dst.at[f ^ 1, q], ssem.at[f, q], rsem.at[f ^ 1, q], nbr[f]).start()

    def outer_sent(q, src, dst, ssem, rsem):
        for f in range(4):
            if f != q:
                @pl.when(jnp.logical_and(has_nb[f], outer[q]))
                def _():
                    remote(src(f, q), dst.at[f ^ 1, q], ssem.at[f, q], rsem.at[f ^ 1, q], nbr[f]).wait_send()

    def on_outer_of_nb(do):
        for f in range(4):
            for q in range(4):
                if q != f ^ 1:
                    @pl.when(jnp.logical_and(has_nb[f], nb_outer[f][q]))
                    def _():
                        do(f, q)

    def outer_received(src, dst, ssem, rsem, do=None):
        def one(f, q):
            remote(src(f, q), dst.at[f, q], ssem.at[f, q], rsem.at[f, q], nbr[f]).wait_recv()
            if do is not None:
                do(f, q)
        on_outer_of_nb(one)

    def basis_face(f):
        return basis.at[f]

    def gather_copies(use):
        return [remote(ebuf.at[use, row], ebuf.at[use, row], es.at[use], er.at[use], (lax.rem(row + d, n_rows), col))
                for d in range(1, n_rows)]

    def gather_wait(use):
        part = ebuf.at[use, pl.ds(0, n_rows - 1)]
        remote(part, part, es.at[use], er.at[use], (lax.rem(row + 1, n_rows), col)).wait()

    def tile_copy(f, slot, half):
        rows = pl.ds(half * (cinv.shape[0] // 2), cinv.shape[0] // 2)
        return remote(cinv.at[rows], nbc.at[slot, rows], cs.at[f, half], cr.at[slot, half], nbr[f])

    def tile_start(half):
        for f in range(2):
            @pl.when(has_nb[f])
            def _():
                tile_copy(f, f ^ 1, half).start()

    def reduce_wait(use, src, dst):
        part = pl.ds(0, n_cols - 1)
        remote(src.at[part], dst.at[part], ps.at[use], pr.at[use], (row, lax.rem(col + 1, n_cols))).wait()

    def reduce_copies(use, src, dst):
        copies = []
        for d in range(1, n_cols):
            c = lax.rem(col + d, n_cols)
            copies.append(remote(src.at[c], dst.at[col], ps.at[use], pr.at[use], (row, c)))
        return copies

    def put_split(ref, x, f):
        hi, lo = split(x)
        ref[0:k, cols_of[f]] = hi
        ref[k:2 * k, cols_of[f]] = lo

    def apply_face(f):
        both = dot(xs[...], ahi[:, cols_of[f]], ((1,), (0,)))
        low = dot(xs[0:k, :], alo[:, cols_of[f]], ((1,), (0,)))
        return both[:k] + (both[k:] + low)

    def expand_face(every, f):
        mine = every[:, 0:mdev]
        theirs = every[:, (1 + f) * mdev:(2 + f) * mdev]
        hi, lo = split(jnp.concatenate([mine, theirs], axis=1))
        wide = jnp.concatenate([jnp.concatenate([hi, hi], axis=1), jnp.concatenate([lo, jnp.zeros_like(lo)], axis=1)], axis=0)
        both = dot(wide, bb[f], ((1,), (0,)))
        return both[:k] + both[k:]

    def restrict_face(x, f):
        return fold(dot(stack(x), bt[f], ((1,), (0,))))

    def a_split(i, carry):
        a_copy(i).wait()
        rows = pl.ds(pl.multiple_of(i * step_rows, step_rows), step_rows)
        hi, lo = split(stage[rows, :])
        ahi[rows, :] = hi
        alo[rows, :] = lo
        return carry

    def put_c(tile, at):
        hi, lo = split(tile.T)
        chi[:, at * modes:(at + 1) * modes] = hi
        clo[:, at * modes:(at + 1) * modes] = lo

    zero_face = jnp.zeros((k, face), F32)
    zero_small = jnp.zeros((k // 2, 2 * mdev), F32)
    for f in range(4):
        @pl.when(outer[f])
        def _():
            nbb[f] = jnp.zeros((mdev, face), F32)
            nbgap[f] = zero_face
            halo_in[f] = zero_face
            nbamps[f] = zero_small
            nbx[f] = zero_small
    pout[0, 3] = zero_small
    pout[n_cols - 1, 4] = zero_small
    chi[:, modes:] = jnp.zeros((chi.shape[0], 2 * modes), BF16)
    clo[:, modes:] = jnp.zeros((chi.shape[0], 2 * modes), BF16)
    for load in loads:
        load.wait()
    ebuf[0, row] = pack(crhs[...])
    for f in range(4):
        contact = jnp.where(has_nb[f], 0, mask[f:f + 1, :])
        cm[f] = jnp.where(contact == 1, 1.0, 0.0).astype(F32)
    put_c(cinv[...], 0)
    early = n_blocks // 4
    lax.fori_loop(0, early, a_split, 0)
    pl.semaphore_wait(barrier, n_dev - 1)

    gathers = gather_copies(0)
    for copy in gathers:
        copy.start()
    for f in range(4):
        face_start(f, basis_face(f), nbb, bs, br)
    lax.fori_loop(early, n_blocks, a_split, 0)
    gather_wait(0)
    gathered = unpack([ebuf[0, r] for r in range(n_rows)])
    partial = dot3(gathered, chi[:, 0:modes], clo[:, 0:modes], ((1,), (0,)))
    for c in range(n_cols):
        pout0[c] = pack(partial[:, c * mdev:(c + 1) * mdev])
    reduces = reduce_copies(0, pout0, pin0)
    for copy in reduces:
        copy.start()
    pin0[col] = pout0[col]
    for f in range(4):
        face_start(f, gap.at[f], nbgap, gs, gr)
        face_start(f, cm, nbcm, ms, mr)
    for f in range(4):
        face_wait(f, basis_face(f), nbb, bs, br)
        both = jnp.concatenate([basis[f], nbb[f]], axis=0)
        hi, lo = split(both)
        bb[f, 0:2 * mdev] = hi
        bb[f, 2 * mdev:4 * mdev] = lo
        hi, lo = split(both.T)
        bt[f, :, 0:2 * mdev] = hi
        bt[f, :, 2 * mdev:4 * mdev] = lo

    def w_cols(g):
        cols = cols_of[g]
        own = jnp.zeros((mdev, face), F32)
        for f in range(4):
            both = dot(bb[f], ahi[cols_of[f], cols], ((1,), (0,)))
            low = dot(bb[f, 0:2 * mdev], alo[cols_of[f], cols], ((1,), (0,)))
            both = both[:2 * mdev] + (both[2 * mdev:] + low)
            own = own + both[:mdev]
            stage[f * mdev:(f + 1) * mdev, cols] = both[mdev:]
            hi, lo = split(both[mdev:])
            whi[(f + 1) * mdev:(f + 2) * mdev, cols] = hi
            wlo[(f + 1) * mdev:(f + 2) * mdev, cols] = lo
        hi, lo = split(own)
        whi[0:mdev, cols] = hi
        wlo[0:mdev, cols] = lo

    w_cols(0)
    w_cols(1)
    reduce_wait(0, pout0, pin0)
    amps = pin0[0]
    for c in range(1, n_cols):
        amps = amps + pin0[c]
    amp_s[...] = amps
    for f in range(4):
        face_start(f, amp_s, nbamps, ams, amr)
    w_cols(2)
    w_cols(3)

    def w_part(f, q):
        return stage.at[f * mdev:(f + 1) * mdev, cols_of[q]]

    mine = jnp.zeros((5 * mdev, mdev), F32)
    theirs = []
    for f in range(4):
        w = jnp.concatenate([whi[:, cols_of[f]], wlo[:, cols_of[f]]], axis=0)
        part = fold(dot(w, bt[f], ((1,), (0,))))
        mine = mine + part[:, 0:mdev]
        theirs.append(part[:, mdev:])
    hi, lo = split(jnp.concatenate([mine] + theirs, axis=1))
    ghi[...] = hi
    glo[...] = lo

    def cross_start(w):
        for f in range(4):
            xbuf[f] = pack(w[:, (1 + f) * mdev:(2 + f) * mdev])
            face_start(f, xbuf.at[f], nbx, xss, xsr)

    def cross_end(w):
        for f in range(4):
            face_wait(f, xbuf.at[f], nbx, xss, xsr)
        total = (nbx[0] + nbx[1]) + (nbx[2] + nbx[3])
        return w[:, 0:mdev] + jnp.concatenate([total[:, :mdev], total[:, mdev:]], axis=0)

    for f in range(4):
        face_wait(f, amp_s, nbamps, ams, amr)
    every = unpack([amp_s[...]] + [nbamps[f] for f in range(4)])
    u = dot3(every, ghi[...], glo[...], ((1,), (0,)))
    cross_start(u)

    def m_face(f, q):
        return m_out.at[q]

    rd = jnp.zeros((k, mdev), F32)
    for f in range(4):
        face_wait(f, gap.at[f], nbgap, gs, gr)
        face_wait(f, cm, nbcm, ms, mr)
        d = gap[f] + nbgap[f]
        dvec[f] = d
        rd = rd + restrict_face(d, f)[:, 0:mdev]
    for f in range(4):
        am[f] = dot3(every, whi[:, cols_of[f]], wlo[:, cols_of[f]], ((1,), (0,)))
    def gather_start():
        ebuf[1, row] = pack(e_s[...])
        for copy in gather_copies(1):
            copy.start()

    e_s[...] = cross_end(u) - rd
    gather_start()
    for f in range(4):
        m_out[f] = expand_face(every, f)

    def put_v(f, q):
        hi, lo = split(vrecv[f, q])
        v[f, q, 0:mdev] = hi
        v[f, q, mdev:2 * mdev] = lo

    lane = lax.broadcasted_iota(jnp.int32, (k, width), 1)
    sub = lax.broadcasted_iota(jnp.int32, (k, width), 0)

    def p_face(f, q):
        return p_out.at[q]

    def sum_copy(src, dst, t):
        return pltpu.make_async_remote_copy(
            src_ref=src, dst_ref=dst, send_sem=rs.at[0], recv_sem=rr.at[0], device_id=t,
            device_id_type=pl.DeviceIdType.LOGICAL)

    sums = sum_copy(red.at[pl.ds(0, n_dev - 1)], red.at[pl.ds(0, n_dev - 1)], others[0])

    p_store = pltpu.make_async_copy(p_out, p_hbm.at[0, 0], out_sem.at[0])

    def iteration(step, ratio):
        @pl.when(step > 0)
        def _():
            for f in range(4):
                @pl.when(has_nb[f])
                def _():
                    m_out[f] = m_out[f] - ratio * p_out[f]
                am[f] = am[f] - ratio * image[f]
            for f in range(4):
                @pl.when(outer[f])
                def _():
                    rows = cols_of[f]
                    change = dxs[:, rows]
                    for g in range(4):
                        both = dot(change, ahi[rows, cols_of[g]], ((1,), (0,)))
                        low = dot(change[0:k], alo[rows, cols_of[g]], ((1,), (0,)))
                        am[g] = am[g] + (both[:k] + (both[k:] + low))

        for f in range(4):
            face_start(f, am.at[f], halo_in, hs, hr)
        gather_wait(1)
        gathered = unpack([ebuf[1, r] for r in range(n_rows)])
        partial = dot3(gathered, chi[...], clo[...], ((1,), (0,)))
        for c in range(n_cols):
            at = [c, n_cols + c, 2 * n_cols + c, c - 1 if c > 0 else None, c + 1 if c < n_cols - 1 else None]
            for i, j in enumerate(at):
                if j is not None:
                    pout[c, i] = pack(partial[:, j * mdev:(j + 1) * mdev])
        copies = reduce_copies(1, pout, pin)
        for copy in copies:
            copy.start()
        pin[col] = pout[col]

        @pl.when(step == 0)
        def _():
            for q in range(4):
                outer_start(q, w_part, vrecv, vs, vr)
                outer_start(q, m_face, nbm, ls, lr)

        @pl.when(step == 1)
        def _():
            tile_start(0)

        @pl.when(step == 2)
        def _():
            tile_start(1)

        squares = jnp.zeros((k, face), F32)
        for f in range(4):
            face_wait(f, am.at[f], halo_in, hs, hr)
            g = am[f] + halo_in[f] - dvec[f]
            grad[f] = g
            put_split(xs, g, f)
            weight = jnp.where(has_nb[f], 0.5, 1.0).astype(F32)
            squares = squares + weight * (g * g)
        numer = jnp.sum(squares, axis=1, keepdims=True)
        squares = jnp.zeros((k, face), F32)
        mine = jnp.zeros((k, mdev), F32)
        theirs = []
        for f in range(4):
            im = apply_face(f)
            image[f] = im
            squares = squares + grad[f] * im
            part = restrict_face(im, f)
            mine = mine + part[:, 0:mdev]
            theirs.append(part[:, mdev:])
        denom = jnp.sum(squares, axis=1, keepdims=True)
        wg = jnp.concatenate([mine] + theirs, axis=1)
        reduce_wait(1, pout, pin)
        total = pin[0]
        for c in range(1, n_cols):
            total = total + pin[c]
        tot[...] = total

        @pl.when(step <= 2)
        def _():
            amp_s[...] = tot[0]
            for f in range(2):
                face_start(f, amp_s, nbamps, ams, amr)
            for f in range(2):
                face_wait(f, amp_s, nbamps, ams, amr)
                tot[1 + f] = nbamps[f]

        every = unpack([tot[i] for i in range(5)])
        wp = wg - dot3(every, ghi[...], glo[...], ((1,), (0,)))
        numer = numer - jnp.sum(e_s[...] * every[:, 0:mdev], axis=1, keepdims=True)
        denom = denom - jnp.sum(every * (wg + wp), axis=1, keepdims=True)
        packed = jnp.where(lane == sub, numer, 0.0) + jnp.where(lane == sub + k, denom, 0.0)
        red[me] = jnp.sum(packed, axis=0, keepdims=True)
        for t in others:
            sum_copy(red.at[me], red.at[me], t).start()
        cross_start(wp)
        for f in range(4):
            p_out[f] = grad[f] - expand_face(every, f)
            outer_start(f, p_face, nbp, qs, qr)
        for f in range(4):
            image[f] = image[f] - dot3(every, whi[:, cols_of[f]], wlo[:, cols_of[f]], ((1,), (0,)))
        @pl.when(step == 0)
        def _():
            outer_received(w_part, vrecv, vs, vr, put_v)
            outer_received(m_face, nbm, ls, lr)
            for q in range(4):
                outer_sent(q, w_part, vrecv, vs, vr)
                outer_sent(q, m_face, nbm, ls, lr)

        @pl.when(step == 2)
        def _():
            for f in range(2):
                @pl.when(has_nb[f])
                def _():
                    for half in range(2):
                        tile_copy(f, f, half).wait()
                    put_c(nbc[f], 1 + f)

        @pl.when(step == ITERS - 1)
        def _():
            p_store.start()

        y = cross_end(wp)
        outer_received(p_face, nbp, qs, qr)
        for q in range(4):
            outer_sent(q, p_face, nbp, qs, qr)
        sums.wait()
        total = jnp.sum(red[...], axis=0)
        numer_all = jnp.sum(jnp.where(lane == sub, total, 0.0), axis=1, keepdims=True)
        denom_all = jnp.sum(jnp.where(lane == sub + k, total, 0.0), axis=1, keepdims=True)
        ratio = numer_all / denom_all
        e_s[...] = e_s[...] - ratio * y

        def clamp(old, p, contact):
            linear = old - ratio * p
            new = jnp.where(contact > 0.5, jnp.maximum(linear, 0.0), linear)
            return new, new - linear

        for f in range(4):
            @pl.when(outer[f])
            def _():
                new, change = clamp(m_out[f], p_out[f], cm[f])
                m_out[f] = new
                put_split(dxs, change, f)

                @pl.when(step < ITERS - 1)
                def _():
                    w = jnp.concatenate([whi[0:mdev, cols_of[f]], wlo[0:mdev, cols_of[f]]], axis=0)
                    e_s[...] = e_s[...] + fold(dot(dxs[:, cols_of[f]], w, ((1,), (1,))))

        def nb_change(f, q):
            new, change = clamp(nbm[f, q], nbp[f, q], nbcm[f, q])
            nbm[f, q] = new
            e_s[...] = e_s[...] + fold(dot(stack(change), v[f, q], ((1,), (1,))))

        @pl.when(step < ITERS - 1)
        def _():
            on_outer_of_nb(nb_change)
            gather_start()

        return ratio

    ratio = lax.fori_loop(0, ITERS, iteration, jnp.zeros((k, 1), F32))
    for f in range(4):
        @pl.when(has_nb[f])
        def _():
            m_out[f] = m_out[f] - ratio * p_out[f]
    m_store = pltpu.make_async_copy(m_out, m_hbm.at[0, 0], out_sem.at[1])
    m_store.start()
    p_store.wait()
    m_store.wait()


def hand_on(m_in, p_in, m_out, p_out):
    m_out[...] = m_in[...]
    p_out[...] = p_in[...]


def solution(mesh):
    n_rows, n_cols = mesh.shape["row"], mesh.shape["col"]

    def shards(dual_ops, basis, coarse_inverse, gap_rhs, coarse_rhs, contact_mask):
        m_len = dual_ops.shape[-1]
        _, _, _, k, face = gap_rhs.shape
        mdev = basis.shape[3]
        width = -(-2 * k // 128) * 128
        blocks = math.gcd(m_len, 32)
        n_dev = n_rows * n_cols
        vm = pltpu.VMEM
        dma = pltpu.SemaphoreType.DMA
        small = (k // 2, 2 * mdev)
        c_rows, c_cols = coarse_inverse.shape
        faces = vm((4, k, face), F32)
        out = jax.ShapeDtypeStruct(gap_rhs.shape, F32)
        anywhere = pl.BlockSpec(memory_space=pl.ANY)
        results = pl.pallas_call(
            functools.partial(kernel, n_rows, n_cols),
            out_shape=(out, out),
            in_specs=[anywhere] * 6,
            out_specs=(anywhere, anywhere),
            scratch_shapes=[
                vm((4, mdev, face), F32), vm(coarse_inverse.shape, F32), faces, vm((k, mdev), F32), vm((4, face), jnp.int32),
                faces, faces,
                vm((m_len, m_len), F32), vm((m_len, m_len), BF16), vm((m_len, m_len), BF16),
                vm((4, 4 * mdev, face), BF16), vm((4, face, 4 * mdev), BF16),
                vm((c_cols, 3 * c_rows), BF16), vm((c_cols, 3 * c_rows), BF16),
                vm((5 * mdev, m_len), BF16), vm((5 * mdev, m_len), BF16),
                vm((5 * mdev, 5 * mdev), BF16), vm((5 * mdev, 5 * mdev), BF16),
                vm((4, 4, 2 * mdev, face), BF16),
                vm((4, mdev, face), F32), faces, faces, faces, faces, faces, faces,
                vm((2 * k, m_len), BF16), vm((2 * k, m_len), BF16), vm((k, mdev), F32),
                vm((2, c_rows, c_cols), F32), vm((4, 4, mdev, face), F32),
                vm((4, 1, face), F32), vm((4, 4, 1, face), F32), vm((4, 4, k, face), F32), vm((4, 4, k, face), F32),
                vm((2, n_rows, *small), F32), vm((n_cols, *small), F32), vm((n_cols, *small), F32),
                vm((n_cols, 5, *small), F32), vm((n_cols, 5, *small), F32),
                vm(small, F32), vm((4, *small), F32), vm((4, *small), F32), vm((4, *small), F32),
                vm((n_dev, 1, width), F32), vm((5, *small), F32),
                dma((5,)), dma((2,)), dma((blocks,)),
                dma((4,)), dma((4,)), dma((4,)), dma((4,)), dma((4,)), dma((4,)),
                dma((2,)), dma((2,)), dma((2,)), dma((2,)),
                dma((4,)), dma((4,)), dma((4,)), dma((4,)), dma((2, 2)), dma((2, 2)), dma((4,)), dma((4,)),
                dma((4, 4)), dma((4, 4)), dma((4, 4)), dma((4, 4)), dma((4, 4)), dma((4, 4)),
                dma((1,)), dma((1,)),
            ],
            compiler_params=pltpu.CompilerParams(
                collective_id=0, has_side_effects=True, vmem_limit_bytes=62 * 1024 * 1024),
        )(dual_ops, basis, coarse_inverse, gap_rhs, coarse_rhs, contact_mask)
        in_vmem = pl.BlockSpec(memory_space=pltpu.VMEM)
        return pl.pallas_call(
            hand_on, out_shape=(out, out), in_specs=[in_vmem] * 2, out_specs=(in_vmem, in_vmem))(*results)

    return jax.shard_map(
        shards,
        mesh=mesh,
        in_specs=(
            P("row", "col", None, None),
            P("row", "col", None, None, None),
            P("row", "col"),
            P("row", "col", None, None, None),
            P("row", "col", None, None),
            P("row", "col", None, None),
        ),
        out_specs=(P("row", "col", None, None, None), P("row", "col", None, None, None)),
        check_vma=False,
    )
```

```python
import functools
import math

import jax
import jax.numpy as jnp
from jax import lax
from jax.experimental import pallas as pl
from jax.experimental.pallas import tpu as pltpu
from jax.sharding import PartitionSpec as P

ITERS = 6
MESH = pl.DeviceIdType.MESH
F32 = jnp.float32
BF16 = jnp.bfloat16


def split(x):
    hi = x.astype(BF16)
    return hi, (x - hi.astype(F32)).astype(BF16)


def dot(a, b, dims):
    return lax.dot_general(a, b, (dims, ((), ())), preferred_element_type=F32)


def dot3(x, hi, lo, dims):
    rows = x.shape[0]
    x_hi, x_lo = split(x)
    both = dot(jnp.concatenate([x_hi, x_lo], axis=0), hi, dims)
    return both[:rows] + (both[rows:] + dot(x_hi, lo, dims))


def fold(out):
    rows, cols = out.shape[0] // 2, out.shape[1] // 2
    return out[:rows, :cols] + (out[rows:, :cols] + out[:rows, cols:])


def stack(x):
    return jnp.concatenate(split(x), axis=0)


def pack(x):
    half = x.shape[0] // 2
    return jnp.concatenate([x[:half], x[half:]], axis=1)


def unpack(parts):
    n = parts[0].shape[1] // 2
    top = jnp.concatenate([p[:, :n] for p in parts], axis=1)
    return jnp.concatenate([top, jnp.concatenate([p[:, n:] for p in parts], axis=1)], axis=0)


def kernel(n_rows, n_cols, a_hbm, basis_hbm, cinv_hbm, gap_hbm, crhs_hbm, mask_hbm, m_hbm, p_hbm,
           basis, cinv, gap, crhs, mask, m_out, p_out,
           stage, ahi, alo, bb, bt, chi, clo, whi, wlo, ghi, glo, v,
           nbb, nbgap, halo_in, am, dvec, grad, image, xs, dxs, e_s, nbc, vrecv, cm, nbcm, nbm, nbp,
           ebuf, pout0, pin0, pout, pin, amp_s, nbamps, xbuf, nbx, red, tot,
           in_sem, out_sem, a_sem, bs, br, gs, gr, hs, hr, es, er, ps, pr, ams, amr, xss, xsr, cs, cr, ms, mr,
           vs, vr, ls, lr, qs, qr, rs, rr):
    row = lax.axis_index("row")
    col = lax.axis_index("col")
    me = row * n_cols + col
    n_dev = n_rows * n_cols
    m_len = ahi.shape[0]
    _, k, face = halo_in.shape
    mdev = nbb.shape[1]
    modes = n_cols * mdev
    width = red.shape[2]
    step_rows = m_len // a_sem.shape[0]
    n_blocks = a_sem.shape[0]
    has_nb = [row > 0, row < n_rows - 1, col > 0, col < n_cols - 1]
    outer = [jnp.logical_not(h) for h in has_nb]
    nbr = [(row - 1, col), (row + 1, col), (row, col - 1), (row, col + 1)]
    nb_outer = [[r == 0, r == n_rows - 1, c == 0, c == n_cols - 1] for r, c in nbr]
    cols_of = [slice(f * face, (f + 1) * face) for f in range(4)]

    def a_copy(i):
        rows = pl.ds(pl.multiple_of(i * step_rows, step_rows), step_rows)
        return pltpu.make_async_copy(a_hbm.at[0, 0, rows], stage.at[rows], a_sem.at[i])

    def a_start(i, carry):
        a_copy(i).start()
        return carry

    loads = [pltpu.make_async_copy(src.at[0, 0], dst, in_sem.at[i]) for i, (src, dst) in enumerate(
        [(crhs_hbm, crhs), (basis_hbm, basis), (mask_hbm, mask), (gap_hbm, gap)])]
    loads.insert(1, pltpu.make_async_copy(cinv_hbm, cinv, in_sem.at[4]))
    for load in loads:
        load.start()
    lax.fori_loop(0, n_blocks, a_start, 0)

    barrier = pltpu.get_barrier_semaphore()
    others = [jnp.where(me + d < n_dev, me + d, me + d - n_dev) for d in range(1, n_dev)]
    for t in others:
        pl.semaphore_signal(barrier, inc=1, device_id=t, device_id_type=pl.DeviceIdType.LOGICAL)

    def remote(src, dst, ssem, rsem, where):
        return pltpu.make_async_remote_copy(
            src_ref=src, dst_ref=dst, send_sem=ssem, recv_sem=rsem, device_id=where, device_id_type=MESH)

    def face_start(f, src, dst, ssem, rsem):
        @pl.when(has_nb[f])
        def _():
            remote(src, dst.at[f ^ 1], ssem.at[f], rsem.at[f ^ 1], nbr[f]).start()

    def face_wait(f, src, dst, ssem, rsem):
        @pl.when(has_nb[f])
        def _():
            remote(src, dst.at[f], ssem.at[f], rsem.at[f], nbr[f]).wait()

    def outer_start(q, src, dst, ssem, rsem):
        for f in range(4):
            if f != q:
                @pl.when(jnp.logical_and(has_nb[f], outer[q]))
                def _():
                    remote(src(f, q), dst.at[f ^ 1, q], ssem.at[f, q], rsem.at[f ^ 1, q], nbr[f]).start()

    def outer_sent(q, src, dst, ssem, rsem):
        for f in range(4):
            if f != q:
                @pl.when(jnp.logical_and(has_nb[f], outer[q]))
                def _():
                    remote(src(f, q), dst.at[f ^ 1, q], ssem.at[f, q], rsem.at[f ^ 1, q], nbr[f]).wait_send()

    def on_outer_of_nb(do):
        for f in range(4):
            for q in range(4):
                if q != f ^ 1:
                    @pl.when(jnp.logical_and(has_nb[f], nb_outer[f][q]))
                    def _():
                        do(f, q)

    def outer_received(src, dst, ssem, rsem, do=None):
        def one(f, q):
            remote(src(f, q), dst.at[f, q], ssem.at[f, q], rsem.at[f, q], nbr[f]).wait_recv()
            if do is not None:
                do(f, q)
        on_outer_of_nb(one)

    def basis_face(f):
        return basis.at[f]

    def gather_copies(use):
        return [remote(ebuf.at[use, row], ebuf.at[use, row], es.at[use], er.at[use], (lax.rem(row + d, n_rows), col))
                for d in range(1, n_rows)]

    def gather_wait(use):
        part = ebuf.at[use, pl.ds(0, n_rows - 1)]
        remote(part, part, es.at[use], er.at[use], (lax.rem(row + 1, n_rows), col)).wait()

    def wide_copy(src, dst, c):
        return remote(pout.at[src], pin.at[dst], ps.at[1], pr.at[1], (row, c))

    def outer_col(c):
        return jnp.logical_or(c == 0, c == n_cols - 1)

    def wide_start():
        for d in range(1, n_cols):
            c = lax.rem(col + d, n_cols)

            @pl.when(outer_col(c))
            def _():
                wide_copy(pl.ds(c * 5, 4), pl.ds(col * 5, 4), c).start()

            @pl.when(jnp.logical_not(outer_col(c)))
            def _():
                wide_copy(pl.ds(c * 5, 5), pl.ds(col * 5, 5), c).start()

    def wide_wait():
        full = 5 * (n_cols - 1)
        if full == 0:
            return
        c = lax.rem(col + 1, n_cols)

        @pl.when(outer_col(col))
        def _():
            wide_copy(pl.ds(0, full - 1), pl.ds(0, full - 1), c).wait_send()
            part = pl.ds(0, full - n_cols + 1)
            wide_copy(part, part, c).wait_recv()

        @pl.when(jnp.logical_not(outer_col(col)))
        def _():
            if n_cols > 2:
                wide_copy(pl.ds(0, full - 2), pl.ds(0, full - 2), c).wait_send()
                wide_copy(pl.ds(0, full), pl.ds(0, full), c).wait_recv()

    def tile_copy(f, slot, half):
        rows = pl.ds(half * (cinv.shape[0] // 2), cinv.shape[0] // 2)
        return remote(cinv.at[rows], nbc.at[slot, rows], cs.at[f, half], cr.at[slot, half], nbr[f])

    def tile_start(half):
        for f in range(2):
            @pl.when(has_nb[f])
            def _():
                tile_copy(f, f ^ 1, half).start()

    def reduce_wait(use, src, dst):
        part = pl.ds(0, n_cols - 1)
        remote(src.at[part], dst.at[part], ps.at[use], pr.at[use], (row, lax.rem(col + 1, n_cols))).wait()

    def reduce_copies(use, src, dst):
        copies = []
        for d in range(1, n_cols):
            c = lax.rem(col + d, n_cols)
            copies.append(remote(src.at[c], dst.at[col], ps.at[use], pr.at[use], (row, c)))
        return copies

    def put_split(ref, x, f):
        hi, lo = split(x)
        ref[0:k, cols_of[f]] = hi
        ref[k:2 * k, cols_of[f]] = lo

    def apply_face(f):
        both = dot(xs[...], ahi[:, cols_of[f]], ((1,), (0,)))
        low = dot(xs[0:k, :], alo[:, cols_of[f]], ((1,), (0,)))
        return both[:k] + (both[k:] + low)

    def expand_face(every, f):
        mine = every[:, 0:mdev]
        theirs = every[:, (1 + f) * mdev:(2 + f) * mdev]
        hi, lo = split(jnp.concatenate([mine, theirs], axis=1))
        wide = jnp.concatenate([jnp.concatenate([hi, hi], axis=1), jnp.concatenate([lo, jnp.zeros_like(lo)], axis=1)], axis=0)
        both = dot(wide, bb[f], ((1,), (0,)))
        return both[:k] + both[k:]

    def restrict_face(x, f):
        return fold(dot(stack(x), bt[f], ((1,), (0,))))

    def a_split(i, carry):
        a_copy(i).wait()
        rows = pl.ds(pl.multiple_of(i * step_rows, step_rows), step_rows)
        hi, lo = split(stage[rows, :])
        ahi[rows, :] = hi
        alo[rows, :] = lo
        return carry

    def put_c(tile, at):
        hi, lo = split(tile.T)
        chi[:, at * modes:(at + 1) * modes] = hi
        clo[:, at * modes:(at + 1) * modes] = lo

    zero_face = jnp.zeros((k, face), F32)
    zero_small = jnp.zeros((k // 2, 2 * mdev), F32)
    for f in range(4):
        @pl.when(outer[f])
        def _():
            nbb[f] = jnp.zeros((mdev, face), F32)
            nbgap[f] = zero_face
            halo_in[f] = zero_face
            nbamps[f] = zero_small
            nbx[f] = zero_small
    for c in range(n_cols):
        pout[c * 5 + 4] = zero_small
        pin[c * 5 + 4] = zero_small
    chi[:, modes:] = jnp.zeros((chi.shape[0], 2 * modes), BF16)
    clo[:, modes:] = jnp.zeros((chi.shape[0], 2 * modes), BF16)
    for load in loads:
        load.wait()
    ebuf[0, row] = pack(crhs[...])
    for f in range(4):
        contact = jnp.where(has_nb[f], 0, mask[f:f + 1, :])
        cm[f] = jnp.where(contact == 1, 1.0, 0.0).astype(F32)
    put_c(cinv[...], 0)
    early = n_blocks // 4
    lax.fori_loop(0, early, a_split, 0)
    pl.semaphore_wait(barrier, n_dev - 1)

    gathers = gather_copies(0)
    for copy in gathers:
        copy.start()
    for f in range(4):
        face_start(f, basis_face(f), nbb, bs, br)
    lax.fori_loop(early, n_blocks, a_split, 0)
    gather_wait(0)
    gathered = unpack([ebuf[0, r] for r in range(n_rows)])
    partial = dot3(gathered, chi[:, 0:modes], clo[:, 0:modes], ((1,), (0,)))
    for c in range(n_cols):
        pout0[c] = pack(partial[:, c * mdev:(c + 1) * mdev])
    reduces = reduce_copies(0, pout0, pin0)
    for copy in reduces:
        copy.start()
    pin0[col] = pout0[col]
    for f in range(4):
        face_start(f, gap.at[f], nbgap, gs, gr)
        face_start(f, cm, nbcm, ms, mr)
    for f in range(4):
        face_wait(f, basis_face(f), nbb, bs, br)
        both = jnp.concatenate([basis[f], nbb[f]], axis=0)
        hi, lo = split(both)
        bb[f, 0:2 * mdev] = hi
        bb[f, 2 * mdev:4 * mdev] = lo
        hi, lo = split(both.T)
        bt[f, :, 0:2 * mdev] = hi
        bt[f, :, 2 * mdev:4 * mdev] = lo

    def w_cols(g):
        cols = cols_of[g]
        own = jnp.zeros((mdev, face), F32)
        for f in range(4):
            both = dot(bb[f], ahi[cols_of[f], cols], ((1,), (0,)))
            low = dot(bb[f, 0:2 * mdev], alo[cols_of[f], cols], ((1,), (0,)))
            both = both[:2 * mdev] + (both[2 * mdev:] + low)
            own = own + both[:mdev]
            stage[f * mdev:(f + 1) * mdev, cols] = both[mdev:]
            hi, lo = split(both[mdev:])
            whi[(f + 1) * mdev:(f + 2) * mdev, cols] = hi
            wlo[(f + 1) * mdev:(f + 2) * mdev, cols] = lo
        hi, lo = split(own)
        whi[0:mdev, cols] = hi
        wlo[0:mdev, cols] = lo

    w_cols(0)
    w_cols(1)
    reduce_wait(0, pout0, pin0)
    amps = pin0[0]
    for c in range(1, n_cols):
        amps = amps + pin0[c]
    amp_s[...] = amps
    for f in range(4):
        face_start(f, amp_s, nbamps, ams, amr)
    w_cols(2)
    w_cols(3)

    def w_part(f, q):
        return stage.at[f * mdev:(f + 1) * mdev, cols_of[q]]

    mine = jnp.zeros((5 * mdev, mdev), F32)
    theirs = []
    for f in range(4):
        w = jnp.concatenate([whi[:, cols_of[f]], wlo[:, cols_of[f]]], axis=0)
        part = fold(dot(w, bt[f], ((1,), (0,))))
        mine = mine + part[:, 0:mdev]
        theirs.append(part[:, mdev:])
    hi, lo = split(jnp.concatenate([mine] + theirs, axis=1))
    ghi[...] = hi
    glo[...] = lo

    def cross_start(w):
        for f in range(4):
            xbuf[f] = pack(w[:, (1 + f) * mdev:(2 + f) * mdev])
            face_start(f, xbuf.at[f], nbx, xss, xsr)

    def cross_end(w):
        for f in range(4):
            face_wait(f, xbuf.at[f], nbx, xss, xsr)
        total = (nbx[0] + nbx[1]) + (nbx[2] + nbx[3])
        return w[:, 0:mdev] + jnp.concatenate([total[:, :mdev], total[:, mdev:]], axis=0)

    for f in range(4):
        face_wait(f, amp_s, nbamps, ams, amr)
    every = unpack([amp_s[...]] + [nbamps[f] for f in range(4)])
    u = dot3(every, ghi[...], glo[...], ((1,), (0,)))
    cross_start(u)

    def m_face(f, q):
        return m_out.at[q]

    rd = jnp.zeros((k, mdev), F32)
    for f in range(4):
        face_wait(f, gap.at[f], nbgap, gs, gr)
        face_wait(f, cm, nbcm, ms, mr)
        d = gap[f] + nbgap[f]
        dvec[f] = d
        rd = rd + restrict_face(d, f)[:, 0:mdev]
    for f in range(4):
        am[f] = dot3(every, whi[:, cols_of[f]], wlo[:, cols_of[f]], ((1,), (0,)))
    def gather_start():
        ebuf[1, row] = pack(e_s[...])
        for copy in gather_copies(1):
            copy.start()

    e_s[...] = cross_end(u) - rd
    gather_start()
    for f in range(4):
        m_out[f] = expand_face(every, f)

    def put_v(f, q):
        hi, lo = split(vrecv[f, q])
        v[f, q, 0:mdev] = hi
        v[f, q, mdev:2 * mdev] = lo

    lane = lax.broadcasted_iota(jnp.int32, (k, width), 1)
    sub = lax.broadcasted_iota(jnp.int32, (k, width), 0)

    def p_face(f, q):
        return p_out.at[q]

    def sum_copy(src, dst, t):
        return pltpu.make_async_remote_copy(
            src_ref=src, dst_ref=dst, send_sem=rs.at[0], recv_sem=rr.at[0], device_id=t,
            device_id_type=pl.DeviceIdType.LOGICAL)

    sums = sum_copy(red.at[pl.ds(0, n_dev - 1)], red.at[pl.ds(0, n_dev - 1)], others[0])

    p_store = pltpu.make_async_copy(p_out, p_hbm.at[0, 0], out_sem.at[0])

    def iteration(step, ratio):
        @pl.when(step > 0)
        def _():
            for f in range(4):
                @pl.when(has_nb[f])
                def _():
                    m_out[f] = m_out[f] - ratio * p_out[f]
                am[f] = am[f] - ratio * image[f]
            for f in range(4):
                @pl.when(outer[f])
                def _():
                    rows = cols_of[f]
                    change = dxs[:, rows]
                    for g in range(4):
                        both = dot(change, ahi[rows, cols_of[g]], ((1,), (0,)))
                        low = dot(change[0:k], alo[rows, cols_of[g]], ((1,), (0,)))
                        am[g] = am[g] + (both[:k] + (both[k:] + low))

        for f in range(4):
            face_start(f, am.at[f], halo_in, hs, hr)
        gather_wait(1)
        gathered = unpack([ebuf[1, r] for r in range(n_rows)])
        partial = dot3(gathered, chi[...], clo[...], ((1,), (0,)))
        for c in range(n_cols):
            sides = [j for j in (c - 1, c + 1) if 0 <= j < n_cols]
            for i, j in enumerate([c, n_cols + c, 2 * n_cols + c] + sides):
                pout[c * 5 + i] = pack(partial[:, j * mdev:(j + 1) * mdev])
        wide_start()
        pin[pl.ds(col * 5, 5)] = pout[pl.ds(col * 5, 5)]

        @pl.when(step == 0)
        def _():
            for q in range(4):
                outer_start(q, w_part, vrecv, vs, vr)
                outer_start(q, m_face, nbm, ls, lr)

        @pl.when(step == 1)
        def _():
            tile_start(0)

        @pl.when(step == 2)
        def _():
            tile_start(1)

        squares = jnp.zeros((k, face), F32)
        for f in range(4):
            face_wait(f, am.at[f], halo_in, hs, hr)
            g = am[f] + halo_in[f] - dvec[f]
            grad[f] = g
            put_split(xs, g, f)
            weight = jnp.where(has_nb[f], 0.5, 1.0).astype(F32)
            squares = squares + weight * (g * g)
        numer = jnp.sum(squares, axis=1, keepdims=True)
        squares = jnp.zeros((k, face), F32)
        mine = jnp.zeros((k, mdev), F32)
        theirs = []
        for f in range(4):
            im = apply_face(f)
            image[f] = im
            squares = squares + grad[f] * im
            part = restrict_face(im, f)
            mine = mine + part[:, 0:mdev]
            theirs.append(part[:, mdev:])
        denom = jnp.sum(squares, axis=1, keepdims=True)
        wg = jnp.concatenate([mine] + theirs, axis=1)
        wide_wait()
        total = pin[0:5]
        for c in range(1, n_cols):
            total = total + pin[c * 5:c * 5 + 5]
        tot[...] = total

        @pl.when(col == 0)
        def _():
            tot[4] = tot[3]
            tot[3] = zero_small


        @pl.when(step <= 2)
        def _():
            amp_s[...] = tot[0]
            for f in range(2):
                face_start(f, amp_s, nbamps, ams, amr)
            for f in range(2):
                face_wait(f, amp_s, nbamps, ams, amr)
                tot[1 + f] = nbamps[f]

        every = unpack([tot[i] for i in range(5)])
        wp = wg - dot3(every, ghi[...], glo[...], ((1,), (0,)))
        numer = numer - jnp.sum(e_s[...] * every[:, 0:mdev], axis=1, keepdims=True)
        denom = denom - jnp.sum(every * (wg + wp), axis=1, keepdims=True)
        packed = jnp.where(lane == sub, numer, 0.0) + jnp.where(lane == sub + k, denom, 0.0)
        red[me] = jnp.sum(packed, axis=0, keepdims=True)
        for t in others:
            sum_copy(red.at[me], red.at[me], t).start()
        cross_start(wp)
        for f in range(4):
            p_out[f] = grad[f] - expand_face(every, f)
            outer_start(f, p_face, nbp, qs, qr)
        for f in range(4):
            image[f] = image[f] - dot3(every, whi[:, cols_of[f]], wlo[:, cols_of[f]], ((1,), (0,)))
        @pl.when(step == 0)
        def _():
            outer_received(w_part, vrecv, vs, vr, put_v)
            outer_received(m_face, nbm, ls, lr)
            for q in range(4):
                outer_sent(q, w_part, vrecv, vs, vr)
                outer_sent(q, m_face, nbm, ls, lr)

        @pl.when(step == 2)
        def _():
            for f in range(2):
                @pl.when(has_nb[f])
                def _():
                    for half in range(2):
                        tile_copy(f, f, half).wait()
                    put_c(nbc[f], 1 + f)

        @pl.when(step == ITERS - 1)
        def _():
            p_store.start()

        y = cross_end(wp)
        outer_received(p_face, nbp, qs, qr)
        for q in range(4):
            outer_sent(q, p_face, nbp, qs, qr)
        sums.wait()
        total = jnp.sum(red[...], axis=0)
        numer_all = jnp.sum(jnp.where(lane == sub, total, 0.0), axis=1, keepdims=True)
        denom_all = jnp.sum(jnp.where(lane == sub + k, total, 0.0), axis=1, keepdims=True)
        ratio = numer_all / denom_all
        e_s[...] = e_s[...] - ratio * y

        def clamp(old, p, contact):
            linear = old - ratio * p
            new = jnp.where(contact > 0.5, jnp.maximum(linear, 0.0), linear)
            return new, new - linear

        for f in range(4):
            @pl.when(outer[f])
            def _():
                new, change = clamp(m_out[f], p_out[f], cm[f])
                m_out[f] = new
                put_split(dxs, change, f)

                @pl.when(step < ITERS - 1)
                def _():
                    w = jnp.concatenate([whi[0:mdev, cols_of[f]], wlo[0:mdev, cols_of[f]]], axis=0)
                    e_s[...] = e_s[...] + fold(dot(dxs[:, cols_of[f]], w, ((1,), (1,))))

        def nb_change(f, q):
            new, change = clamp(nbm[f, q], nbp[f, q], nbcm[f, q])
            nbm[f, q] = new
            e_s[...] = e_s[...] + fold(dot(stack(change), v[f, q], ((1,), (1,))))

        @pl.when(step < ITERS - 1)
        def _():
            on_outer_of_nb(nb_change)
            gather_start()

        return ratio

    ratio = lax.fori_loop(0, ITERS, iteration, jnp.zeros((k, 1), F32))
    for f in range(4):
        @pl.when(has_nb[f])
        def _():
            m_out[f] = m_out[f] - ratio * p_out[f]
    m_store = pltpu.make_async_copy(m_out, m_hbm.at[0, 0], out_sem.at[1])
    m_store.start()
    p_store.wait()
    m_store.wait()


def hand_on(m_in, p_in, m_out, p_out):
    m_out[...] = m_in[...]
    p_out[...] = p_in[...]


def solution(mesh):
    n_rows, n_cols = mesh.shape["row"], mesh.shape["col"]

    def shards(dual_ops, basis, coarse_inverse, gap_rhs, coarse_rhs, contact_mask):
        m_len = dual_ops.shape[-1]
        _, _, _, k, face = gap_rhs.shape
        mdev = basis.shape[3]
        width = -(-2 * k // 128) * 128
        blocks = math.gcd(m_len, 32)
        n_dev = n_rows * n_cols
        vm = pltpu.VMEM
        dma = pltpu.SemaphoreType.DMA
        small = (k // 2, 2 * mdev)
        c_rows, c_cols = coarse_inverse.shape
        faces = vm((4, k, face), F32)
        out = jax.ShapeDtypeStruct(gap_rhs.shape, F32)
        anywhere = pl.BlockSpec(memory_space=pl.ANY)
        results = pl.pallas_call(
            functools.partial(kernel, n_rows, n_cols),
            out_shape=(out, out),
            in_specs=[anywhere] * 6,
            out_specs=(anywhere, anywhere),
            scratch_shapes=[
                vm((4, mdev, face), F32), vm(coarse_inverse.shape, F32), faces, vm((k, mdev), F32), vm((4, face), jnp.int32),
                faces, faces,
                vm((m_len, m_len), F32), vm((m_len, m_len), BF16), vm((m_len, m_len), BF16),
                vm((4, 4 * mdev, face), BF16), vm((4, face, 4 * mdev), BF16),
                vm((c_cols, 3 * c_rows), BF16), vm((c_cols, 3 * c_rows), BF16),
                vm((5 * mdev, m_len), BF16), vm((5 * mdev, m_len), BF16),
                vm((5 * mdev, 5 * mdev), BF16), vm((5 * mdev, 5 * mdev), BF16),
                vm((4, 4, 2 * mdev, face), BF16),
                vm((4, mdev, face), F32), faces, faces, faces, faces, faces, faces,
                vm((2 * k, m_len), BF16), vm((2 * k, m_len), BF16), vm((k, mdev), F32),
                vm((2, c_rows, c_cols), F32), vm((4, 4, mdev, face), F32),
                vm((4, 1, face), F32), vm((4, 4, 1, face), F32), vm((4, 4, k, face), F32), vm((4, 4, k, face), F32),
                vm((2, n_rows, *small), F32), vm((n_cols, *small), F32), vm((n_cols, *small), F32),
                vm((n_cols * 5, *small), F32), vm((n_cols * 5, *small), F32),
                vm(small, F32), vm((4, *small), F32), vm((4, *small), F32), vm((4, *small), F32),
                vm((n_dev, 1, width), F32), vm((5, *small), F32),
                dma((5,)), dma((2,)), dma((blocks,)),
                dma((4,)), dma((4,)), dma((4,)), dma((4,)), dma((4,)), dma((4,)),
                dma((2,)), dma((2,)), dma((2,)), dma((2,)),
                dma((4,)), dma((4,)), dma((4,)), dma((4,)), dma((2, 2)), dma((2, 2)), dma((4,)), dma((4,)),
                dma((4, 4)), dma((4, 4)), dma((4, 4)), dma((4, 4)), dma((4, 4)), dma((4, 4)),
                dma((1,)), dma((1,)),
            ],
            compiler_params=pltpu.CompilerParams(
                collective_id=0, has_side_effects=True, vmem_limit_bytes=62 * 1024 * 1024),
        )(dual_ops, basis, coarse_inverse, gap_rhs, coarse_rhs, contact_mask)
        in_vmem = pl.BlockSpec(memory_space=pltpu.VMEM)
        return pl.pallas_call(
            hand_on, out_shape=(out, out), in_specs=[in_vmem] * 2, out_specs=(in_vmem, in_vmem))(*results)

    return jax.shard_map(
        shards,
        mesh=mesh,
        in_specs=(
            P("row", "col", None, None),
            P("row", "col", None, None, None),
            P("row", "col"),
            P("row", "col", None, None, None),
            P("row", "col", None, None),
            P("row", "col", None, None),
        ),
        out_specs=(P("row", "col", None, None, None), P("row", "col", None, None, None)),
        check_vma=False,
    )
```
